512 devices in a mesh: ctx: 32 (over z_lo, x), tp: 8 (over y, core), dp: 2 (over z_hi).
Axes of the slice: x: 4, y: 4, z: 16 (z_hi: 2, z_lo: 8; z = z_hi * 8 + z_lo), core: 2. Of those that a mesh axis runs over, the one named last changes fastest.
Arguments:
- query: bfloat16 [2, 4096, 3072], P('dp', 'ctx', 'tp'), may hold values from -6 to 6
- key: bfloat16 [2, 4096, 3072], P('dp', 'ctx', 'tp'), may hold values from -6 to 6
- value: bfloat16 [2, 4096, 3072], P('dp', 'ctx', 'tp'), may hold values from -8 to 8
- w_out: bfloat16 [3072, 3072], P('tp'), may hold values from -0.109375 to 0.109375
- output_gradient: bfloat16 [2, 4096, 3072], P('dp', ('ctx', 'tp')), may hold values from -3 to 3
- key_blocks: int32 [2, 32, 17], P('dp'), may hold values from -1 to 31, as said below
- band_ids: int32 [2, 4096], P('dp', 'ctx'), may hold values from 0 to 5
- band_bias: float32 [24, 6, 6], P('tp'), may hold values from -1.5 to 1.5
Outputs:
- attn_out: bfloat16 [2, 4096, 3072], P('dp', ('ctx', 'tp'))
- grad_query: bfloat16 [2, 4096, 3072], P('dp', 'ctx', 'tp')
- grad_key: bfloat16 [2, 4096, 3072], P('dp', 'ctx', 'tp')
- grad_value: bfloat16 [2, 4096, 3072], P('dp', 'ctx', 'tp')
- grad_bias: float32 [24, 6, 6], P('tp')
The draws below stay inside these ranges and needn't reach their ends.
Inputs may be any that keep to these rules, and one draw needn't show every extreme that they name: `key_blocks`: row b of a sequence holds distinct key block numbers from b - 16 to b, b itself first, then -1 to the end; how many are listed varies from row to row, and the last block of each sequence lists 17.
All inputs are finite; a program needn't handle non-finite values.
Results may differ from the reference program's by a relative error of at most 0.02.
Values may be sent and summed in bfloat16 or wider, within the bound.
A program may use at most 128 MiB of HBM per device.

```python
import math
import jax
import jax.numpy as jnp
from jax import lax

D = 3072
HEADS = 24
HEAD = 128
NBANDS = 6
BLK = 128
SEQS = 2
SEQ_LEN = 4096
NBLK = 32
KWIN = 17
HD = 3072


def draw_query(key, part):
    own_key = jax.random.fold_in(key, 21)
    base = jnp.clip(1.5 * jax.random.normal(own_key, (SEQS, SEQ_LEN, HD), jnp.float32), -6.0, 6.0)
    return base.astype(jnp.bfloat16)


def draw_key(key, part):
    own_key = jax.random.fold_in(key, 22)
    base = jnp.clip(1.5 * jax.random.normal(own_key, (SEQS, SEQ_LEN, HD), jnp.float32), -6.0, 6.0)
    return base.astype(jnp.bfloat16)


def draw_key_blocks(key, part):
    offsets = jnp.arange(KWIN, dtype=jnp.int32)[None, None, :]
    blocks = jnp.arange(NBLK, dtype=jnp.int32)[None, :, None]
    raw = jax.random.randint(jax.random.fold_in(key, 31), (SEQS, NBLK, KWIN), 0, 4096)
    score = raw * KWIN + offsets
    score = jnp.where(offsets == 0, -1, score)
    score = jnp.where(offsets > blocks, 4096 * KWIN + offsets, score)
    order = jnp.argsort(score, axis=-1, stable=True).astype(jnp.int32)
    counts = jax.random.randint(jax.random.fold_in(key, 32), (SEQS, NBLK, 1), 1, KWIN + 1)
    counts = jnp.minimum(counts, blocks + 1)
    counts = jnp.where(blocks == NBLK - 1, KWIN, counts)
    return jnp.where(offsets < counts, blocks - order, -1).astype(jnp.int32)


def place_ends(entries, rng, smallest, top_value):
    extent = entries.shape
    spot = [jax.random.randint(jax.random.fold_in(rng, axis), (), 0, extent[axis]) for axis in range(len(extent))]
    entries = entries.at[tuple(spot)].set(smallest)
    longest = extent.index(max(extent))
    spot[longest] = (spot[longest] + 1) % extent[longest]
    return entries.at[tuple(spot)].set(top_value)


def level_of(rng, extent, cuts, smallest, high):
    level = 1.0
    for dim, blocks in cuts:
        draws = jax.random.uniform(jax.random.fold_in(jax.random.fold_in(rng, 6), dim), (blocks,), jnp.float32, smallest / len(cuts), high / len(cuts))
        level = level * jnp.repeat(jnp.exp(draws), extent[dim] // blocks).reshape((-1,) + (1,) * (len(extent) - 1 - dim))
    return level


def gaussian(key, extent, deviation, most, shards=(), held_as=jnp.bfloat16):
    values = deviation * jax.random.normal(key, extent, jnp.float32)
    if shards:
        values = values * level_of(key, extent, shards, -0.22, 0.18)
    return jnp.clip(values, -most, most).astype(held_as)


def setup_inputs(seed: int = 0) -> dict:
    seeds = jax.random.split(jax.random.key(seed), 9)
    return {
        "query": draw_query(jax.random.fold_in(seeds[8], 71), 0),
        "key": draw_key(jax.random.fold_in(seeds[8], 71), 0),
        "value": gaussian(seeds[2], (SEQS, SEQ_LEN, HD), 2.0, 8.0, ((0, 2), (1, 32), (2, 8))),
        "w_out": gaussian(seeds[3], (HD, D), HD ** -0.5, 0.109375, ((0, 8),)),
        "output_gradient": gaussian(seeds[4], (SEQS, SEQ_LEN, D), 0.5, 3.0, ((0, 2), (1, 256))),
        "key_blocks": draw_key_blocks(jax.random.fold_in(seeds[8], 71), 0),
        "band_ids": place_ends(jax.random.randint(seeds[6], (SEQS, SEQ_LEN), 0, NBANDS), jax.random.fold_in(seeds[6], 1), 0, NBANDS - 1).astype(jnp.int32),
        "band_bias": jnp.clip(jax.random.uniform(seeds[7], (HEADS, NBANDS, NBANDS), jnp.float32, -1.5, 1.5) * level_of(seeds[7], (HEADS, NBANDS, NBANDS), ((0, 8),), -0.4, 0.0), -1.5, 1.5),
    }


def to_half(value_rows):
    return lax.optimization_barrier(value_rows.astype(jnp.bfloat16)).astype(jnp.float32)

def windowed(rows, source):
    shaped = rows.reshape((NBLK, BLK) + rows.shape[1:])
    padding = jnp.zeros((KWIN - 1,) + shaped.shape[1:], rows.dtype)
    return jnp.concatenate([padding, shaped], axis=0)[source]

def unwindow(parts, source):
    total = jnp.zeros((NBLK + KWIN - 1,) + parts.shape[2:], jnp.float32)
    total = total.at[source].add(parts)
    return total[KWIN - 1:].reshape((SEQ_LEN,) + parts.shape[3:])

def one_hot_bands(bands):
    return (bands[..., None] == jnp.arange(NBANDS, dtype=jnp.int32)).astype(jnp.float32)

def split_heads(rows):
    return rows.reshape(SEQ_LEN, HEADS, HEAD).transpose(1, 0, 2)

def join_heads(rows):
    return rows.transpose(1, 0, 2).reshape(SEQ_LEN, HD)

def reference(query, key, value, w_out, output_gradient, key_blocks, band_ids, band_bias):
    scale = 1.0 / math.sqrt(HEAD)
    offsets = jnp.arange(KWIN, dtype=jnp.int32)
    blocks = jnp.arange(NBLK, dtype=jnp.int32)
    target = (blocks[:, None] - offsets[None, :]).astype(jnp.int32)
    source = (target + (KWIN - 1)).astype(jnp.int32)
    outputs = []
    grads_q = []
    grads_k = []
    grads_v = []
    bias_total = jnp.zeros((HEADS, NBANDS, NBANDS), jnp.float32)
    for seq in range(SEQS):
        lists = key_blocks[seq]
        allowed = jnp.any(lists[:, None, :] == target[:, :, None], axis=-1) & (target >= 0)
        bands = band_ids[seq]
        band_rows = bands.reshape(NBLK, BLK)
        band_cols = windowed(bands, source)
        left_operand = one_hot_bands(band_rows)
        right_operand = one_hot_bands(band_cols)
        grad_att = jnp.dot(output_gradient[seq], w_out.T, preferred_element_type=jnp.float32).astype(jnp.bfloat16)

        def per_head(items):
            q_head, k_head, v_head, g_head, lookup_table = items
            q_four = q_head.reshape(NBLK, BLK, HEAD).astype(jnp.float32)
            k_win = windowed(k_head, source).astype(jnp.float32)
            v_win = windowed(v_head, source).astype(jnp.float32)
            bias = lookup_table[band_rows[:, :, None, None], band_cols[:, None, :, :]]
            scores = jnp.einsum('qid,qjkd->qijk', q_four, k_win) * scale + bias
            scores = jnp.where(allowed[:, None, :, None], scores, -jnp.inf)
            top = lax.optimization_barrier(jnp.max(scores, axis=(2, 3), keepdims=True))
            expo = jnp.exp(scores - top)
            total = lax.optimization_barrier(jnp.sum(expo, axis=(2, 3), keepdims=True))
            mixed = jnp.einsum('qijk,qjkd->qid', to_half(expo), v_win)
            attended = (mixed / total[:, :, :, 0]).astype(jnp.bfloat16)
            log_total = top + jnp.log(total)
            g_four = g_head.reshape(NBLK, BLK, HEAD).astype(jnp.float32)
            delta = lax.optimization_barrier(jnp.sum(g_four * attended.astype(jnp.float32), axis=-1))
            prob = jnp.exp(scores - log_total)
            dprob = jnp.einsum('qid,qjkd->qijk', g_four, v_win)
            dscore = prob * (dprob - delta[:, :, None, None])
            grad_b = jnp.einsum('qia,qijk,qjkb->ab', left_operand, dscore, right_operand, precision=lax.Precision.HIGHEST)
            dscore_half = to_half(dscore)
            grad_q = (jnp.einsum('qijk,qjkd->qid', dscore_half, k_win) * scale).astype(jnp.bfloat16)
            k_parts = jnp.einsum('qijk,qid->qjkd', dscore_half, q_four) * scale
            v_parts = jnp.einsum('qijk,qid->qjkd', to_half(prob), g_four)
            grad_k = unwindow(k_parts, source).astype(jnp.bfloat16)
            grad_v = unwindow(v_parts, source).astype(jnp.bfloat16)
            return (attended.reshape(SEQ_LEN, HEAD), grad_q.reshape(SEQ_LEN, HEAD), grad_k, grad_v, grad_b)
        attended, grad_q, grad_k, grad_v, grad_b = lax.map(per_head, (split_heads(query[seq]), split_heads(key[seq]), split_heads(value[seq]), split_heads(grad_att), band_bias))
        outputs.append(jnp.dot(join_heads(attended), w_out, preferred_element_type=jnp.float32).astype(jnp.bfloat16))
        grads_q.append(join_heads(grad_q))
        grads_k.append(join_heads(grad_k))
        grads_v.append(join_heads(grad_v))
        bias_total = bias_total + grad_b
    return (jnp.stack(outputs), jnp.stack(grads_q), jnp.stack(grads_k), jnp.stack(grads_v), bias_total)
```

```python
import functools
import math

import jax
import jax.numpy as jnp
from jax import lax
from jax.experimental import pallas as pl
from jax.experimental.pallas import tpu as pltpu
from jax.sharding import PartitionSpec as P

HEAD = 128
BLK = 128
NX = 4
NZ = 8
MESH = pl.DeviceIdType.MESH
F32 = jnp.float32
BF16 = jnp.bfloat16
NT = (((1,), (1,)), ((), ()))
NN = (((1,), (0,)), ((), ()))


def dot(a, b, dims, precision=None):
    return lax.dot_general(a, b, dims, preferred_element_type=F32, precision=precision)


def remote(src, dst, send, recv, axis, index):
    return pltpu.make_async_remote_copy(
        src_ref=src,
        dst_ref=dst,
        send_sem=send,
        recv_sem=recv,
        device_id={axis: index},
        device_id_type=MESH,
    )


def exchange_kernel(
    kvb, qb, og, w_hbm, kvw, qbw, gw, cot, wv, gown,
    send, recv, cot_send, cot_recv, local
):
    c = lax.axis_index("ctx")
    t = lax.axis_index("tp")
    x = lax.rem(c, NX)
    z = c // NX
    tps = cot.shape[0]
    wcopy = pltpu.make_async_copy(w_hbm, wv, local.at[0])
    wcopy.start()

    barrier = pltpu.get_barrier_semaphore()
    for dx in range(1, NX):
        peer = z * NX + lax.rem(x + dx, NX)
        pl.semaphore_signal(barrier, inc=1, device_id={"ctx": peer}, device_id_type=MESH)
    for dt in range(1, tps):
        pl.semaphore_signal(
            barrier, inc=1, device_id={"tp": lax.rem(t + dt, tps)}, device_id_type=MESH
        )

    @pl.when(z > 0)
    def _():
        pl.semaphore_signal(barrier, inc=1, device_id={"ctx": c - NX}, device_id_type=MESH)

    @pl.when(z < NZ - 1)
    def _():
        pl.semaphore_signal(barrier, inc=1, device_id={"ctx": c + NX}, device_id_type=MESH)

    neighbours = jnp.where((z > 0) & (z < NZ - 1), 2, 1)
    pl.semaphore_wait(barrier, NX - 1 + tps - 1 + neighbours)

    streams = ((kvb, kvw, True), (qb, qbw, False), (gown, gw, False))

    def row_copy(n, dx):
        own, window, _ = streams[n]
        peer = z * NX + lax.rem(x + NX - dx, NX)
        return remote(own, window.at[0, dx], send.at[n, 0, dx], recv.at[n, 0, dx], "ctx", peer)

    def hop_copy(n, s, dx):
        own, window, up = streams[n]
        source = own if (s == 1 and dx == 0) else window.at[s - 1, dx]
        peer = jnp.clip(c + NX if up else c - NX, 0, NX * NZ - 1)
        return remote(source, window.at[s, dx], send.at[n, s, dx], recv.at[n, s, dx], "ctx", peer)

    def edge(n, dx):
        if streams[n][2]:
            return x + dx < NX
        return (x + dx >= NX) if dx else (x >= 0)

    def sends(n, s, dx):
        if streams[n][2]:
            cond = (z >= s - 1) & (z < NZ - 1)
        else:
            cond = (z + (s - 1) < NZ) & (z > 0)
        return cond & edge(n, dx) if s == NX else cond

    def receives(n, s, dx):
        cond = (z >= s) if streams[n][2] else (z + s < NZ)
        return cond & edge(n, dx) if s == NX else cond

    def wait_arrival(n, s, dx):
        if s == 0:
            if dx:
                row_copy(n, dx).wait_recv()
        else:

            @pl.when(receives(n, s, dx))
            def _():
                hop_copy(n, s, dx).wait_recv()

    def start_rows(n):
        for dx in range(1, NX):
            row_copy(n, dx).start()

    def hop(n, s):
        for dx in range(NX):
            wait_arrival(n, s - 1, dx)

            @pl.when(sends(n, s, dx))
            def _():
                hop_copy(n, s, dx).start()

    def cot_copy(dt):
        peer = lax.rem(t + tps - dt, tps)
        return remote(og, cot.at[t], cot_send.at[dt], cot_recv.at[dt], "tp", peer)

    def cot_arrival(dt):
        peer = lax.rem(t + dt, tps)
        return remote(og, cot.at[peer], cot_send.at[dt], cot_recv.at[dt], "tp", peer)

    for dt in range(1, tps):
        cot_copy(dt).start()
    start_rows(0)
    start_rows(1)
    own_kv = pltpu.make_async_copy(kvb, kvw.at[0, 0], local.at[1])
    own_kv.start()
    own_q = pltpu.make_async_copy(qb, qbw.at[0, 0], local.at[2])
    own_q.start()
    cot[t] = og[...]
    hop(0, 1)
    hop(1, 1)
    for dt in range(1, tps):
        cot_arrival(dt).wait_recv()
    wcopy.wait()
    rows = cot.shape[0] * cot.shape[1]
    gown[...] = dot(cot[...].reshape(rows, cot.shape[2]), wv[...], NT).astype(BF16)
    own_g = pltpu.make_async_copy(gown, gw.at[0, 0], local.at[3])
    own_g.start()
    start_rows(2)
    for s in range(2, NX + 1):
        hop(0, s)
        hop(1, s)
        hop(2, s - 1)
    hop(2, NX)
    for n in range(3):
        for dx in range(NX):
            wait_arrival(n, NX, dx)
    for dt in range(1, tps):
        cot_copy(dt).wait_send()
    for n in range(3):
        for dx in range(1, NX):
            row_copy(n, dx).wait_send()
        for s in range(1, NX + 1):
            for dx in range(NX):

                @pl.when(sends(n, s, dx))
                def _():
                    hop_copy(n, s, dx).wait_send()

    own_kv.wait()
    own_q.wait()
    own_g.wait()


def head_cols(h):
    return pl.ds(h * HEAD, HEAD)


def band_hits(band_row, rows, shift=None):
    r = lax.broadcasted_iota(jnp.int32, (rows, BLK), 0)
    want = band_row.astype(jnp.int32)
    if shift is None:
        hit = (r & 7) == want
    else:
        hit = r == want + shift
    return hit.astype(F32).astype(BF16)


def query_kernel(
    heads, meta, kvw, qb, gw, ext, w_out, out, grad_q, stats, bias, s_buf, m_buf, l_buf, acc, rsum, att
):
    scale = 1.0 / math.sqrt(HEAD)
    count = s_buf.shape[0]
    m_buf[...] = jnp.full_like(m_buf, -jnp.inf)
    l_buf[...] = jnp.zeros_like(l_buf)
    acc[...] = jnp.zeros_like(acc)
    rsum[...] = jnp.zeros_like(rsum)

    def first(j, carry):
        @pl.when(meta[0, j] == 1)
        def _():
            s, dx = meta[1, j], meta[2, j]
            hits = band_hits(kvw[s, dx, 2 * BLK : 2 * BLK + 16, 0:BLK].astype(F32)[0:1], 32)
            for h in range(heads):
                k_h = kvw[s, dx, 0:BLK, head_cols(h)]
                score = dot(qb[0:BLK, head_cols(h)], k_h, NT) * scale + dot(ext[h], hits, NN)
                s_buf[j, h] = score
                m_buf[h] = jnp.maximum(m_buf[h], score)

        return carry

    lax.fori_loop(0, count, first, 0)
    for h in range(heads):
        m_buf[h] = jnp.broadcast_to(jnp.max(m_buf[h], axis=1, keepdims=True), (BLK, BLK))

    def second(j, carry):
        @pl.when(meta[0, j] == 1)
        def _():
            s, dx = meta[1, j], meta[2, j]
            for h in range(heads):
                v_h = kvw[s, dx, BLK : 2 * BLK, head_cols(h)]
                expo = jnp.exp(s_buf[j, h] - m_buf[h])
                l_buf[h] += expo
                acc[h] += dot(expo.astype(BF16), v_h, NN)

        return carry

    lax.fori_loop(0, count, second, 0)
    lane = lax.broadcasted_iota(jnp.int32, (BLK, BLK), 1)
    table = jnp.zeros((BLK, BLK), F32)
    for h in range(heads):
        total = jnp.sum(l_buf[h], axis=1, keepdims=True)
        attended = (acc[h] / total).astype(BF16)
        att[:, head_cols(h)] = attended
        lse = m_buf[h] + jnp.log(total)
        g_h = gw[0:BLK, head_cols(h)].astype(F32)
        delta = jnp.sum(g_h * attended.astype(F32), axis=1, keepdims=True)
        m_buf[h] = lse
        l_buf[h] = jnp.broadcast_to(delta, (BLK, BLK))
        table = jnp.where(lane == h, lse, table)
        table = jnp.where(lane == heads + h, l_buf[h], table)
        acc[h] = jnp.zeros((BLK, HEAD), F32)
    stats[...] = jnp.transpose(table)[0:8]
    out[...] = dot(att[...], w_out[...], NN).astype(BF16)

    def third(j, carry):
        @pl.when(meta[0, j] == 1)
        def _():
            s, dx = meta[1, j], meta[2, j]
            band_row = kvw[s, dx, 2 * BLK : 2 * BLK + 16, 0:BLK].astype(F32)[0:1]
            for h in range(heads):
                k_h = kvw[s, dx, 0:BLK, head_cols(h)]
                v_h = kvw[s, dx, BLK : 2 * BLK, head_cols(h)]
                prob = jnp.exp(s_buf[j, h] - m_buf[h])
                dprob = dot(gw[0:BLK, head_cols(h)], v_h, NT)
                dscore = prob * (dprob - l_buf[h])
                half = dscore.astype(BF16)
                rest = (dscore - half.astype(F32)).astype(BF16)
                acc[h] += dot(half, k_h, NN)
                hits = band_hits(band_row, BLK, 8 * h)
                rsum[...] += dot(half, hits, NT) + dot(rest, hits, NT)

        return carry

    lax.fori_loop(0, count, third, 0)
    for h in range(heads):
        grad_q[:, head_cols(h)] = (acc[h] * scale).astype(BF16)
    own = qb[BLK : BLK + 16, 0:BLK].astype(F32)[0:1].astype(jnp.int32)
    pick = (lax.broadcasted_iota(jnp.int32, (8, BLK), 0) == own).astype(F32)
    bias[...] = dot(pick, rsum[...], NN, lax.Precision.HIGHEST)


def share_kernel(
    partial, stats, bias, pieces, window, total, bx, bz, bd, mid, top,
    p_send, p_recv, s_send, s_recv, b_send, b_recv, local
):
    c = lax.axis_index("ctx")
    t = lax.axis_index("tp")
    d = lax.axis_index("dp")
    x = lax.rem(c, NX)
    z = c // NX
    tps = partial.shape[0]
    count = window.shape[0]
    ring = NX * NZ
    barrier = pltpu.get_barrier_semaphore()
    for dc in range(1, ring):
        pl.semaphore_signal(
            barrier, inc=1, device_id={"ctx": lax.rem(c + dc, ring)}, device_id_type=MESH
        )
    for dt in range(1, tps):
        pl.semaphore_signal(
            barrier, inc=1, device_id={"tp": lax.rem(t + dt, tps)}, device_id_type=MESH
        )
    pl.semaphore_signal(barrier, inc=1, device_id={"dp": 1 - d}, device_id_type=MESH)
    pl.semaphore_wait(barrier, ring - 1 + tps - 1 + 1)

    def piece_copy(dt):
        peer = lax.rem(t + dt, tps)
        return remote(partial.at[peer], pieces.at[dt], p_send.at[dt], p_recv.at[dt], "tp", peer)

    def stat_copy(j):
        peer = jnp.clip(c - j, 0, ring - 1)
        return remote(stats, window.at[j], s_send.at[j], s_recv.at[j], "ctx", peer)

    def x_copy(dx, slot):
        peer = z * NX + lax.rem(x + dx, NX)
        return remote(bias, bx.at[slot], b_send.at[0, dx], b_recv.at[0, dx], "ctx", peer)

    def z_copy(dz, slot):
        peer = lax.rem(z + dz, NZ) * NX + x
        return remote(mid, bz.at[slot], b_send.at[1, dz], b_recv.at[1, dz], "ctx", peer)

    for dx in range(1, NX):
        x_copy(dx, x).start()
    for j in range(1, count):

        @pl.when(c >= j)
        def _():
            stat_copy(j).start()

    for dt in range(1, tps):
        piece_copy(dt).start()
    own_piece = pltpu.make_async_copy(partial.at[t], pieces.at[0], local.at[0])
    own_piece.start()
    window[0] = stats[...]
    bx[x] = bias[...]
    for dx in range(1, NX):
        x_copy(dx, lax.rem(x + NX - dx, NX)).wait_recv()
    mid[...] = (bx[0] + bx[1]) + (bx[2] + bx[3])
    for dz in range(1, NZ):
        z_copy(dz, z).start()
    bz[z] = mid[...]
    for dz in range(1, NZ):
        z_copy(dz, lax.rem(z + NZ - dz, NZ)).wait_recv()
    acc = bz[0]
    for i in range(1, NZ):
        acc = acc + bz[i]
    top[...] = acc
    cross = remote(top, bd, b_send.at[2, 0], b_recv.at[2, 0], "dp", 1 - d)
    cross.start()
    for j in range(1, count):

        @pl.when(c + j < ring)
        def _():
            stat_copy(j).wait_recv()

    for dt in range(1, tps):
        piece_copy(dt).wait_recv()
    cross.wait_recv()
    total[...] = top[...] + bd[...]
    for dx in range(1, NX):
        x_copy(dx, x).wait_send()
    for dz in range(1, NZ):
        z_copy(dz, z).wait_send()
    for j in range(1, count):

        @pl.when(c >= j)
        def _():
            stat_copy(j).wait_send()

    for dt in range(1, tps):
        piece_copy(dt).wait_send()
    cross.wait_send()
    own_piece.wait()


def key_kernel(heads, meta, kvb, ext, qbw, gw, stats, pieces, attn, grad_k, grad_v, dk, dv):
    scale = 1.0 / math.sqrt(HEAD)
    count = stats.shape[0]
    dk[...] = jnp.zeros_like(dk)
    dv[...] = jnp.zeros_like(dv)
    acc = pieces[0].astype(F32)
    for i in range(1, pieces.shape[0]):
        acc = acc + pieces[i].astype(F32)
    attn[...] = acc.astype(BF16)

    def step(j, carry):
        @pl.when(meta[3, j] == 1)
        def _():
            s, dx = meta[4, j], meta[5, j]
            hits = band_hits(qbw[s, dx, BLK : BLK + 16, 0:BLK].astype(F32)[0:1], 32)
            rows = stats[j]
            for h in range(heads):
                q_h = qbw[s, dx, 0:BLK, head_cols(h)]
                g_h = gw[s, dx, :, head_cols(h)]
                k_h = kvb[0:BLK, head_cols(h)]
                v_h = kvb[BLK : 2 * BLK, head_cols(h)]
                score = dot(k_h, q_h, NT) * scale + dot(ext[h], hits, NN)
                prob = jnp.exp(score - rows[h : h + 1])
                dprob = dot(v_h, g_h, NT)
                dscore = prob * (dprob - rows[heads + h : heads + h + 1])
                dk[h] += dot(dscore.astype(BF16), q_h, NN)
                dv[h] += dot(prob.astype(BF16), g_h, NN)

        return carry

    lax.fori_loop(0, count, step, 0)
    for h in range(heads):
        grad_k[:, head_cols(h)] = (dk[h] * scale).astype(BF16)
        grad_v[:, head_cols(h)] = dv[h].astype(BF16)


def split_bands(values):
    parts = []
    rest = values
    for _ in range(3):
        part = lax.reduce_precision(rest, 8, 7)
        parts.append(part)
        rest = rest - part
    stacked = jnp.stack(parts, axis=2)
    stacked = jnp.pad(stacked, ((0, 0), (0, 0), (0, 1), (0, 8 - values.shape[2])))
    return stacked.reshape(values.shape[0], values.shape[1], 32).astype(BF16)


def body(query, key, value, w_out, output_gradient, key_blocks, band_ids, band_bias):
    q_rows, k_rows, v_rows, og = query[0], key[0], value[0], output_gradient[0]
    bands, lists = band_ids[0], key_blocks[0]
    rows, feats = q_rows.shape
    heads = band_bias.shape[0]
    nblk, window = lists.shape
    width = og.shape[1]
    tps = lax.axis_size("tp")
    c = lax.axis_index("ctx")
    band_rows = jnp.pad(bands.astype(BF16)[None, :], ((0, 15), (0, feats - rows)))
    kvb = jnp.concatenate([k_rows, v_rows, band_rows], axis=0)
    qb = jnp.concatenate([q_rows, band_rows], axis=0)
    one_hot = (bands[:, None] == jnp.arange(band_bias.shape[1], dtype=jnp.int32)).astype(F32)
    high = lax.Precision.HIGHEST
    ext_q = split_bands(jnp.einsum("ia,hab->hib", one_hot, band_bias, precision=high))
    ext_k = split_bands(jnp.einsum("kb,hab->hka", one_hot, band_bias, precision=high))
    steps = jnp.arange(window, dtype=jnp.int32)
    keys = c - steps
    queries = c + steps
    own_list = lax.dynamic_index_in_dim(lists, c, 0, keepdims=False)
    allow_q = jnp.any(own_list[None, :] == keys[:, None], axis=1) & (keys >= 0)
    later = lax.dynamic_slice_in_dim(
        jnp.pad(lists, ((0, window), (0, 0)), constant_values=-1), c, window, 0
    )
    allow_k = jnp.any(later == c, axis=1) & (queries < nblk)
    place = lambda blocks: (jnp.abs(c // NX - blocks // NX), lax.rem(blocks % NX + NX - c % NX, NX))
    keys_in = jnp.where(allow_q, keys, c)
    queries_in = jnp.where(allow_k, queries, c)
    table = jnp.stack(
        [allow_q.astype(jnp.int32), *place(keys_in), allow_k.astype(jnp.int32), *place(queries_in)]
    )

    vmem = pl.BlockSpec(memory_space=pltpu.VMEM)
    smem = pl.BlockSpec(memory_space=pltpu.SMEM)
    hbm = pl.BlockSpec(memory_space=pl.ANY)
    shape = jax.ShapeDtypeStruct
    kvw, qbw, gw = pl.pallas_call(
        exchange_kernel,
        out_shape=(
            shape((NX + 1, NX) + kvb.shape, BF16),
            shape((NX + 1, NX) + qb.shape, BF16),
            shape((NX + 1, NX, rows, feats), BF16),
        ),
        in_specs=[vmem, vmem, vmem, hbm],
        out_specs=(hbm, hbm, hbm),
        scratch_shapes=[
            pltpu.VMEM((tps,) + og.shape, BF16),
            pltpu.VMEM(w_out.shape, BF16),
            pltpu.VMEM((rows, feats), BF16),
            pltpu.SemaphoreType.DMA((3, NX + 1, NX)),
            pltpu.SemaphoreType.DMA((3, NX + 1, NX)),
            pltpu.SemaphoreType.DMA((tps,)),
            pltpu.SemaphoreType.DMA((tps,)),
            pltpu.SemaphoreType.DMA((4,)),
        ],
        compiler_params=pltpu.CompilerParams(collective_id=0, has_side_effects=True),
        name="exchange",
    )(kvb, qb, og, w_out)

    square = pltpu.VMEM((heads, BLK, BLK), F32)
    partial, grad_q, stats, bias = pl.pallas_call(
        functools.partial(query_kernel, heads),
        out_shape=(
            shape((rows, width), BF16),
            shape((rows, feats), BF16),
            shape((8, BLK), F32),
            shape((8, BLK), F32),
        ),
        in_specs=[smem] + [vmem] * 5,
        out_specs=(vmem,) * 4,
        scratch_shapes=[
            pltpu.VMEM((window, heads, BLK, BLK), F32),
            square,
            square,
            square,
            pltpu.VMEM((BLK, BLK), F32),
            pltpu.VMEM((rows, feats), BF16),
        ],
        name="query_side",
    )(table, kvw, qb, gw[0, 0], ext_q, w_out)

    tile = (8, BLK)
    pieces, stat_window, bias_total = pl.pallas_call(
        share_kernel,
        out_shape=(
            shape((tps,) + og.shape, BF16),
            shape((window,) + tile, F32),
            shape(tile, F32),
        ),
        in_specs=[vmem] * 3,
        out_specs=(vmem,) * 3,
        scratch_shapes=[
            pltpu.VMEM((NX,) + tile, F32),
            pltpu.VMEM((NZ,) + tile, F32),
            pltpu.VMEM(tile, F32),
            pltpu.VMEM(tile, F32),
            pltpu.VMEM(tile, F32),
            pltpu.SemaphoreType.DMA((tps,)),
            pltpu.SemaphoreType.DMA((tps,)),
            pltpu.SemaphoreType.DMA((window,)),
            pltpu.SemaphoreType.DMA((window,)),
            pltpu.SemaphoreType.DMA((3, NZ)),
            pltpu.SemaphoreType.DMA((3, NZ)),
            pltpu.SemaphoreType.DMA((1,)),
        ],
        compiler_params=pltpu.CompilerParams(collective_id=1, has_side_effects=True),
        name="share",
    )(partial.reshape((tps,) + og.shape), stats, bias)

    attn_out, grad_k, grad_v = pl.pallas_call(
        functools.partial(key_kernel, heads),
        out_shape=(shape(og.shape, BF16), shape((rows, feats), BF16), shape((rows, feats), BF16)),
        in_specs=[smem] + [vmem] * 6,
        out_specs=(vmem,) * 3,
        scratch_shapes=[square, square],
        name="key_side",
    )(table, kvb, ext_k, qbw, gw, stat_window, pieces)

    na, nb = band_bias.shape[1:]
    grad_bias = bias_total[:na, : 8 * heads].reshape(na, heads, 8)[:, :, :nb].transpose(1, 0, 2)
    return (attn_out[None], grad_q[None], grad_k[None], grad_v[None], grad_bias)


def solution(mesh):
    return jax.shard_map(
        body,
        mesh=mesh,
        in_specs=(
            P("dp", "ctx", "tp"),
            P("dp", "ctx", "tp"),
            P("dp", "ctx", "tp"),
            P("tp", None),
            P("dp", ("ctx", "tp"), None),
            P("dp", None, None),
            P("dp", "ctx"),
            P("tp", None, None),
        ),
        out_specs=(
            P("dp", ("ctx", "tp"), None),
            P("dp", "ctx", "tp"),
            P("dp", "ctx", "tp"),
            P("dp", "ctx", "tp"),
            P("tp", None, None),
        ),
        check_vma=False,
    )
```

```python
import functools
import math

import jax
import jax.numpy as jnp
from jax import lax
from jax.experimental import pallas as pl
from jax.experimental.pallas import tpu as pltpu
from jax.sharding import PartitionSpec as P

HEAD = 128
BLK = 128
NX = 4
NZ = 8
TURN = 1
MESH = pl.DeviceIdType.MESH
F32 = jnp.float32
BF16 = jnp.bfloat16
NT = (((1,), (1,)), ((), ()))
NN = (((1,), (0,)), ((), ()))


def dot(a, b, dims, precision=None):
    return lax.dot_general(a, b, dims, preferred_element_type=F32, precision=precision)


def remote(src, dst, send, recv, axis, index):
    return pltpu.make_async_remote_copy(
        src_ref=src,
        dst_ref=dst,
        send_sem=send,
        recv_sem=recv,
        device_id={axis: index},
        device_id_type=MESH,
    )


def exchange_kernel(
    q, k, v, band_rows, og, w_hbm, kvw, qbw, gw, gown, kvb, qb, cot, wv,
    send, recv, cot_send, cot_recv, local
):
    c = lax.axis_index("ctx")
    t = lax.axis_index("tp")
    x = lax.rem(c, NX)
    z = c // NX
    tps = cot.shape[0]
    wcopy = pltpu.make_async_copy(w_hbm, wv, local.at[0])
    wcopy.start()
    kvb[0:BLK] = k[...]
    kvb[BLK : 2 * BLK] = v[...]
    kvb[2 * BLK :] = band_rows[...]
    qb[0:BLK] = q[...]
    qb[BLK:] = band_rows[...]

    barrier = pltpu.get_barrier_semaphore()
    for dx in range(1, NX):
        peer = z * NX + lax.rem(x + dx, NX)
        pl.semaphore_signal(barrier, inc=1, device_id={"ctx": peer}, device_id_type=MESH)
    for dt in range(1, tps):
        pl.semaphore_signal(
            barrier, inc=1, device_id={"tp": lax.rem(t + dt, tps)}, device_id_type=MESH
        )

    @pl.when(z > 0)
    def _():
        pl.semaphore_signal(barrier, inc=1, device_id={"ctx": c - NX}, device_id_type=MESH)

    @pl.when(z < NZ - 1)
    def _():
        pl.semaphore_signal(barrier, inc=1, device_id={"ctx": c + NX}, device_id_type=MESH)

    neighbours = jnp.where((z > 0) & (z < NZ - 1), 2, 1)
    pl.semaphore_wait(barrier, NX - 1 + tps - 1 + neighbours)

    streams = ((kvb, kvw, True), (qb, qbw, False), (gown, gw, False))

    def row_copy(n, dx):
        own, window, _ = streams[n]
        peer = z * NX + lax.rem(x + NX - dx, NX)
        return remote(own, window.at[0, dx], send.at[n, 0, dx], recv.at[n, 0, dx], "ctx", peer)

    def hop_copy(n, s, dx):
        own, window, up = streams[n]
        sems = send.at[n, s, dx], recv.at[n, s, dx], "ctx"
        if dx == TURN:
            peer = z * NX + lax.rem(x + NX - dx, NX)
            return remote(window.at[s, 0], window.at[s, dx], *sems, peer)
        source = own if (s == 1 and dx == 0) else window.at[s - 1, dx]
        peer = jnp.clip(c + NX if up else c - NX, 0, NX * NZ - 1)
        return remote(source, window.at[s, dx], *sems, peer)

    def edge(n, dx, place):
        if streams[n][2]:
            return place + dx < NX
        return (place + dx >= NX) if dx else (place >= 0)

    def sends(n, s, dx):
        up = streams[n][2]
        if dx == TURN:
            cond = (z >= s) if up else (z + s < NZ)
            target = lax.rem(x + NX - dx, NX)
        else:
            cond = ((z >= s - 1) & (z < NZ - 1)) if up else ((z + (s - 1) < NZ) & (z > 0))
            target = x
        return cond & edge(n, dx, target) if s == NX else cond

    def receives(n, s, dx):
        cond = (z >= s) if streams[n][2] else (z + s < NZ)
        return cond & edge(n, dx, x) if s == NX else cond

    def wait_arrival(n, s, dx):
        if s == 0:
            if dx:
                row_copy(n, dx).wait_recv()
        else:

            @pl.when(receives(n, s, dx))
            def _():
                hop_copy(n, s, dx).wait_recv()

    def start_rows(n):
        for dx in range(1, NX):
            row_copy(n, dx).start()

    def start_hop(n, s, dx):
        @pl.when(sends(n, s, dx))
        def _():
            hop_copy(n, s, dx).start()

    def hop(n, s):
        for dx in range(NX):
            if dx != TURN:
                wait_arrival(n, s - 1, dx)
                start_hop(n, s, dx)
                if dx == 0 and s > 1:
                    start_hop(n, s - 1, TURN)

    def cot_copy(dt):
        peer = lax.rem(t + tps - dt, tps)
        return remote(og, cot.at[t], cot_send.at[dt], cot_recv.at[dt], "tp", peer)

    def cot_arrival(dt):
        peer = lax.rem(t + dt, tps)
        return remote(og, cot.at[peer], cot_send.at[dt], cot_recv.at[dt], "tp", peer)

    for dt in range(1, tps):
        cot_copy(dt).start()
    start_rows(0)
    start_rows(1)
    own_kv = pltpu.make_async_copy(kvb, kvw.at[0, 0], local.at[1])
    own_kv.start()
    own_q = pltpu.make_async_copy(qb, qbw.at[0, 0], local.at[2])
    own_q.start()
    cot[t] = og[...]
    hop(0, 1)
    hop(1, 1)
    for dt in range(1, tps):
        cot_arrival(dt).wait_recv()
    wcopy.wait()
    rows = cot.shape[0] * cot.shape[1]
    gown[...] = dot(cot[...].reshape(rows, cot.shape[2]), wv[...], NT).astype(BF16)
    own_g = pltpu.make_async_copy(gown, gw.at[0, 0], local.at[3])
    own_g.start()
    start_rows(2)
    hop(2, 1)
    for s in range(2, NX + 1):
        for n in range(3):
            hop(n, s)
    for n in range(3):
        wait_arrival(n, NX, 0)
        start_hop(n, NX, TURN)
    for n in range(3):
        for dx in range(1, NX):
            if dx == TURN:
                for s in range(NX):
                    wait_arrival(n, s, dx)
            wait_arrival(n, NX, dx)
    for dt in range(1, tps):
        cot_copy(dt).wait_send()
    for n in range(3):
        for dx in range(1, NX):
            row_copy(n, dx).wait_send()
        for s in range(1, NX + 1):
            for dx in range(NX):

                @pl.when(sends(n, s, dx))
                def _():
                    hop_copy(n, s, dx).wait_send()

    own_kv.wait()
    own_q.wait()
    own_g.wait()


def head_cols(h):
    return pl.ds(h * HEAD, HEAD)


def band_hits(band_row, rows, shift=None):
    r = lax.broadcasted_iota(jnp.int32, (rows, BLK), 0)
    want = band_row.astype(jnp.int32)
    if shift is None:
        hit = (r & 7) == want
    else:
        hit = r == want + shift
    return hit.astype(F32).astype(BF16)


def query_kernel(
    heads, meta, kvw, qb, band_rows, gw, ext, w_out, out, grad_q, stats, bias, s_buf, m_buf, l_buf, acc, rsum, att
):
    scale = 1.0 / math.sqrt(HEAD)
    count = s_buf.shape[0]
    m_buf[...] = jnp.full_like(m_buf, -jnp.inf)
    l_buf[...] = jnp.zeros_like(l_buf)
    acc[...] = jnp.zeros_like(acc)
    rsum[...] = jnp.zeros_like(rsum)

    def first(j, carry):
        @pl.when(meta[0, j] == 1)
        def _():
            s, dx = meta[1, j], meta[2, j]
            hits = band_hits(kvw[s, dx, 2 * BLK : 2 * BLK + 16, 0:BLK].astype(F32)[0:1], 32)
            for h in range(heads):
                k_h = kvw[s, dx, 0:BLK, head_cols(h)]
                score = dot(qb[0:BLK, head_cols(h)], k_h, NT) * scale + dot(ext[h], hits, NN)
                s_buf[j, h] = score
                m_buf[h] = jnp.maximum(m_buf[h], score)

        return carry

    lax.fori_loop(0, count, first, 0)
    for h in range(heads):
        m_buf[h] = jnp.broadcast_to(jnp.max(m_buf[h], axis=1, keepdims=True), (BLK, BLK))

    def second(j, carry):
        @pl.when(meta[0, j] == 1)
        def _():
            s, dx = meta[1, j], meta[2, j]
            for h in range(heads):
                v_h = kvw[s, dx, BLK : 2 * BLK, head_cols(h)]
                expo = jnp.exp(s_buf[j, h] - m_buf[h])
                l_buf[h] += expo
                acc[h] += dot(expo.astype(BF16), v_h, NN)

        return carry

    lax.fori_loop(0, count, second, 0)
    lane = lax.broadcasted_iota(jnp.int32, (BLK, BLK), 1)
    table = jnp.zeros((BLK, BLK), F32)
    for h in range(heads):
        total = jnp.sum(l_buf[h], axis=1, keepdims=True)
        attended = (acc[h] / total).astype(BF16)
        att[:, head_cols(h)] = attended
        lse = m_buf[h] + jnp.log(total)
        g_h = gw[0:BLK, head_cols(h)].astype(F32)
        delta = jnp.sum(g_h * attended.astype(F32), axis=1, keepdims=True)
        m_buf[h] = lse
        l_buf[h] = jnp.broadcast_to(delta, (BLK, BLK))
        table = jnp.where(lane == h, lse, table)
        table = jnp.where(lane == heads + h, l_buf[h], table)
        acc[h] = jnp.zeros((BLK, HEAD), F32)
    stats[...] = jnp.transpose(table)[0:8]
    out[...] = dot(att[...], w_out[...], NN).astype(BF16)

    def third(j, carry):
        @pl.when(meta[0, j] == 1)
        def _():
            s, dx = meta[1, j], meta[2, j]
            band_row = kvw[s, dx, 2 * BLK : 2 * BLK + 16, 0:BLK].astype(F32)[0:1]
            for h in range(heads):
                k_h = kvw[s, dx, 0:BLK, head_cols(h)]
                v_h = kvw[s, dx, BLK : 2 * BLK, head_cols(h)]
                prob = jnp.exp(s_buf[j, h] - m_buf[h])
                dprob = dot(gw[0:BLK, head_cols(h)], v_h, NT)
                dscore = prob * (dprob - l_buf[h])
                half = dscore.astype(BF16)
                rest = (dscore - half.astype(F32)).astype(BF16)
                acc[h] += dot(half, k_h, NN)
                hits = band_hits(band_row, BLK, 8 * h)
                rsum[...] += dot(half, hits, NT) + dot(rest, hits, NT)

        return carry

    lax.fori_loop(0, count, third, 0)
    for h in range(heads):
        grad_q[:, head_cols(h)] = (acc[h] * scale).astype(BF16)
    own = band_rows[:, 0:BLK].astype(F32)[0:1].astype(jnp.int32)
    pick = (lax.broadcasted_iota(jnp.int32, (8, BLK), 0) == own).astype(F32)
    bias[...] = dot(pick, rsum[...], NN, lax.Precision.HIGHEST)


def share_kernel(
    heads, veto, partial, stats, bias, k, v, ext, qbw, gw, attn, grad_k, grad_v, total,
    pieces, window, bx, bz, bd, mid, top, qv, gv, dk, dv,
    p_send, p_recv, s_send, s_recv, b_send, b_recv, local
):
    c = lax.axis_index("ctx")
    t = lax.axis_index("tp")
    d = lax.axis_index("dp")
    x = lax.rem(c, NX)
    z = c // NX
    tps = partial.shape[0]
    count = window.shape[0]
    ring = NX * NZ
    scale = 1.0 / math.sqrt(HEAD)
    q_load = pltpu.make_async_copy(qbw, qv, local.at[1])
    q_load.start()
    g_load = pltpu.make_async_copy(gw, gv, local.at[2])
    g_load.start()
    dk[...] = jnp.zeros_like(dk)
    dv[...] = jnp.zeros_like(dv)
    barrier = pltpu.get_barrier_semaphore()
    for dc in range(1, ring):
        pl.semaphore_signal(
            barrier, inc=1, device_id={"ctx": lax.rem(c + dc, ring)}, device_id_type=MESH
        )
    for dt in range(1, tps):
        pl.semaphore_signal(
            barrier, inc=1, device_id={"tp": lax.rem(t + dt, tps)}, device_id_type=MESH
        )
    pl.semaphore_signal(barrier, inc=1, device_id={"dp": 1 - d}, device_id_type=MESH)
    pl.semaphore_wait(barrier, ring - 1 + tps - 1 + 1)

    def piece_copy(dt):
        peer = lax.rem(t + dt, tps)
        return remote(partial.at[peer], pieces.at[dt], p_send.at[dt], p_recv.at[dt], "tp", peer)

    def stat_copy(j):
        peer = jnp.clip(c - j, 0, ring - 1)
        return remote(stats, window.at[j], s_send.at[j], s_recv.at[j], "ctx", peer)

    def x_copy(dx, slot):
        peer = z * NX + lax.rem(x + dx, NX)
        return remote(bias, bx.at[slot], b_send.at[0, dx], b_recv.at[0, dx], "ctx", peer)

    def z_copy(dz, slot):
        peer = lax.rem(z + dz, NZ) * NX + x
        return remote(mid, bz.at[slot], b_send.at[1, dz], b_recv.at[1, dz], "ctx", peer)

    for dx in range(1, NX):
        x_copy(dx, x).start()
    for j in range(1, count):

        @pl.when(c >= j)
        def _():
            stat_copy(j).start()

    for dt in range(1, tps):
        piece_copy(dt).start()
    own_piece = pltpu.make_async_copy(partial.at[t], pieces.at[0], local.at[0])
    own_piece.start()
    window[0] = stats[...]
    bx[x] = bias[...]
    for dx in range(1, NX):
        x_copy(dx, lax.rem(x + NX - dx, NX)).wait_recv()
    mid[...] = (bx[0] + bx[1]) + (bx[2] + bx[3])
    for dz in range(1, NZ):
        z_copy(dz, z).start()
    bz[z] = mid[...]
    for j in range(1, count):

        @pl.when(c + j < ring)
        def _():
            stat_copy(j).wait_recv()

    q_load.wait()
    g_load.wait()

    def step(j, carry):
        @pl.when(c + j < ring)
        def _():
            s, dx = (x + j) // NX, lax.rem(j, NX)
            hits = band_hits(qv[s, dx, BLK : BLK + 16, 0:BLK].astype(F32)[0:1], 32)
            rows = window[j]
            for h in range(heads):
                q_h = qv[s, dx, 0:BLK, head_cols(h)]
                g_h = gv[s, dx, :, head_cols(h)]
                k_h = k[:, head_cols(h)]
                v_h = v[:, head_cols(h)]
                score = dot(k_h, q_h, NT) * scale + dot(ext[h], hits, NN)
                prob = jnp.exp(score - (rows[h : h + 1] + veto[j]))
                dprob = dot(v_h, g_h, NT)
                dscore = prob * (dprob - rows[heads + h : heads + h + 1])
                dk[h] += dot(dscore.astype(BF16), q_h, NN)
                dv[h] += dot(prob.astype(BF16), g_h, NN)

        return carry

    lax.fori_loop(0, count // 2, step, 0)
    for dz in range(1, NZ):
        z_copy(dz, lax.rem(z + NZ - dz, NZ)).wait_recv()
    acc = bz[0]
    for i in range(1, NZ):
        acc = acc + bz[i]
    top[...] = acc
    cross = remote(top, bd, b_send.at[2, 0], b_recv.at[2, 0], "dp", 1 - d)
    cross.start()
    lax.fori_loop(count // 2, count, step, 0)
    for h in range(heads):
        grad_k[:, head_cols(h)] = (dk[h] * scale).astype(BF16)
        grad_v[:, head_cols(h)] = dv[h].astype(BF16)
    own_piece.wait()
    for dt in range(1, tps):
        piece_copy(dt).wait_recv()
    out = pieces[0].astype(F32)
    for i in range(1, tps):
        out = out + pieces[i].astype(F32)
    attn[...] = out.astype(BF16)
    cross.wait_recv()
    total[...] = top[...] + bd[...]
    for dx in range(1, NX):
        x_copy(dx, x).wait_send()
    for dz in range(1, NZ):
        z_copy(dz, z).wait_send()
    for j in range(1, count):

        @pl.when(c >= j)
        def _():
            stat_copy(j).wait_send()

    for dt in range(1, tps):
        piece_copy(dt).wait_send()
    cross.wait_send()


def split_bands(values):
    parts = []
    rest = values
    for _ in range(3):
        part = lax.reduce_precision(rest, 8, 7)
        parts.append(part)
        rest = rest - part
    stacked = jnp.stack(parts, axis=2)
    stacked = jnp.pad(stacked, ((0, 0), (0, 0), (0, 1), (0, 8 - values.shape[2])))
    return stacked.reshape(values.shape[0], values.shape[1], 32).astype(BF16)


def body(query, key, value, w_out, output_gradient, key_blocks, band_ids, band_bias):
    q_rows, k_rows, v_rows, og = query[0], key[0], value[0], output_gradient[0]
    bands, lists = band_ids[0], key_blocks[0]
    rows, feats = q_rows.shape
    heads = band_bias.shape[0]
    nblk, window = lists.shape
    width = og.shape[1]
    tps = lax.axis_size("tp")
    c = lax.axis_index("ctx")
    band_rows = jnp.pad(bands.astype(BF16)[None, :], ((0, 15), (0, feats - rows)))
    one_hot = (bands[:, None] == jnp.arange(band_bias.shape[1], dtype=jnp.int32)).astype(F32)
    high = lax.Precision.HIGHEST
    ext_q = split_bands(jnp.einsum("ia,hab->hib", one_hot, band_bias, precision=high))
    ext_k = split_bands(jnp.einsum("kb,hab->hka", one_hot, band_bias, precision=high))
    steps = jnp.arange(window, dtype=jnp.int32)
    keys = c - steps
    queries = c + steps
    own_list = lax.dynamic_index_in_dim(lists, c, 0, keepdims=False)
    allow_q = jnp.any(own_list[None, :] == keys[:, None], axis=1) & (keys >= 0)
    later = lax.dynamic_slice_in_dim(
        jnp.pad(lists, ((0, window), (0, 0)), constant_values=-1), c, window, 0
    )
    allow_k = jnp.any(later == c, axis=1) & (queries < nblk)
    keys_in = jnp.where(allow_q, keys, c)
    row_gap = c // NX - keys_in // NX
    column_gap = lax.rem(keys_in % NX + NX - c % NX, NX)
    table = jnp.stack([allow_q.astype(jnp.int32), row_gap, column_gap])
    veto = jnp.where(allow_k, 0.0, 1e30).astype(F32)

    vmem = pl.BlockSpec(memory_space=pltpu.VMEM)
    smem = pl.BlockSpec(memory_space=pltpu.SMEM)
    hbm = pl.BlockSpec(memory_space=pl.ANY)
    shape = jax.ShapeDtypeStruct
    kv_shape = (2 * rows + 16, feats)
    qb_shape = (rows + 16, feats)
    kvw, qbw, gw, grad_att = pl.pallas_call(
        exchange_kernel,
        out_shape=(
            shape((NX + 1, NX) + kv_shape, BF16),
            shape((NX + 1, NX) + qb_shape, BF16),
            shape((NX + 1, NX, rows, feats), BF16),
            shape((rows, feats), BF16),
        ),
        in_specs=[vmem] * 5 + [hbm],
        out_specs=(hbm, hbm, hbm, vmem),
        scratch_shapes=[
            pltpu.VMEM(kv_shape, BF16),
            pltpu.VMEM(qb_shape, BF16),
            pltpu.VMEM((tps,) + og.shape, BF16),
            pltpu.VMEM(w_out.shape, BF16),
            pltpu.SemaphoreType.DMA((3, NX + 1, NX)),
            pltpu.SemaphoreType.DMA((3, NX + 1, NX)),
            pltpu.SemaphoreType.DMA((tps,)),
            pltpu.SemaphoreType.DMA((tps,)),
            pltpu.SemaphoreType.DMA((4,)),
        ],
        compiler_params=pltpu.CompilerParams(collective_id=0, has_side_effects=True),
        name="exchange",
    )(q_rows, k_rows, v_rows, band_rows, og, w_out)

    square = pltpu.VMEM((heads, BLK, BLK), F32)
    partial, grad_q, stats, bias = pl.pallas_call(
        functools.partial(query_kernel, heads),
        out_shape=(
            shape((rows, width), BF16),
            shape((rows, feats), BF16),
            shape((8, BLK), F32),
            shape((8, BLK), F32),
        ),
        in_specs=[smem] + [vmem] * 6,
        out_specs=(vmem,) * 4,
        scratch_shapes=[
            pltpu.VMEM((window, heads, BLK, BLK), F32),
            square,
            square,
            square,
            pltpu.VMEM((BLK, BLK), F32),
            pltpu.VMEM((rows, feats), BF16),
        ],
        name="query_side",
    )(table, kvw, q_rows, band_rows, grad_att, ext_q, w_out)

    tile = (8, BLK)
    attn_out, grad_k, grad_v, bias_total = pl.pallas_call(
        functools.partial(share_kernel, heads),
        out_shape=(
            shape(og.shape, BF16),
            shape((rows, feats), BF16),
            shape((rows, feats), BF16),
            shape(tile, F32),
        ),
        in_specs=[smem] + [vmem] * 6 + [hbm] * 2,
        out_specs=(vmem,) * 4,
        scratch_shapes=[
            pltpu.VMEM((tps,) + og.shape, BF16),
            pltpu.VMEM((window,) + tile, F32),
            pltpu.VMEM((NX,) + tile, F32),
            pltpu.VMEM((NZ,) + tile, F32),
            pltpu.VMEM(tile, F32),
            pltpu.VMEM(tile, F32),
            pltpu.VMEM(tile, F32),
            pltpu.VMEM(qbw.shape, BF16),
            pltpu.VMEM(gw.shape, BF16),
            square,
            square,
            pltpu.SemaphoreType.DMA((tps,)),
            pltpu.SemaphoreType.DMA((tps,)),
            pltpu.SemaphoreType.DMA((window,)),
            pltpu.SemaphoreType.DMA((window,)),
            pltpu.SemaphoreType.DMA((3, NZ)),
            pltpu.SemaphoreType.DMA((3, NZ)),
            pltpu.SemaphoreType.DMA((3,)),
        ],
        compiler_params=pltpu.CompilerParams(collective_id=1, has_side_effects=True),
        name="share",
    )(
        veto, partial.reshape((tps,) + og.shape), stats, bias,
        k_rows, v_rows, ext_k, qbw, gw,
    )

    na, nb = band_bias.shape[1:]
    grad_bias = bias_total[:na, : 8 * heads].reshape(na, heads, 8)[:, :, :nb].transpose(1, 0, 2)
    return (attn_out[None], grad_q[None], grad_k[None], grad_v[None], grad_bias)


def solution(mesh):
    return jax.shard_map(
        body,
        mesh=mesh,
        in_specs=(
            P("dp", "ctx", "tp"),
            P("dp", "ctx", "tp"),
            P("dp", "ctx", "tp"),
            P("tp", None),
            P("dp", ("ctx", "tp"), None),
            P("dp", None, None),
            P("dp", "ctx"),
            P("tp", None, None),
        ),
        out_specs=(
            P("dp", ("ctx", "tp"), None),
            P("dp", "ctx", "tp"),
            P("dp", "ctx", "tp"),
            P("dp", "ctx", "tp"),
            P("tp", None, None),
        ),
        check_vma=False,
    )
```

```python
import functools
import math

import jax
import jax.numpy as jnp
from jax import lax
from jax.experimental import pallas as pl
from jax.experimental.pallas import tpu as pltpu
from jax.sharding import PartitionSpec as P

HEAD = 128
BLK = 128
NX = 4
NZ = 8
TURN = 1
UNROLL = 3
MESH = pl.DeviceIdType.MESH
F32 = jnp.float32
BF16 = jnp.bfloat16
NT = (((1,), (1,)), ((), ()))
NN = (((1,), (0,)), ((), ()))


def dot(a, b, dims, precision=None):
    return lax.dot_general(a, b, dims, preferred_element_type=F32, precision=precision)


def remote(src, dst, send, recv, axis, index):
    return pltpu.make_async_remote_copy(
        src_ref=src,
        dst_ref=dst,
        send_sem=send,
        recv_sem=recv,
        device_id={axis: index},
        device_id_type=MESH,
    )


def exchange_kernel(
    q, k, v, band_rows, og, w_hbm, kvw, qbw, gw, gown, kvb, qb, cot, wv,
    send, recv, cot_send, cot_recv, local
):
    c = lax.axis_index("ctx")
    t = lax.axis_index("tp")
    x = lax.rem(c, NX)
    z = c // NX
    tps = cot.shape[0]
    wcopy = pltpu.make_async_copy(w_hbm, wv, local.at[0])
    wcopy.start()
    kvb[0:BLK] = k[...]
    kvb[BLK : 2 * BLK] = v[...]
    kvb[2 * BLK :] = band_rows[...]
    qb[0:BLK] = q[...]
    qb[BLK:] = band_rows[...]

    barrier = pltpu.get_barrier_semaphore()
    for dx in range(1, NX):
        peer = z * NX + lax.rem(x + dx, NX)
        pl.semaphore_signal(barrier, inc=1, device_id={"ctx": peer}, device_id_type=MESH)
    for dt in range(1, tps):
        pl.semaphore_signal(
            barrier, inc=1, device_id={"tp": lax.rem(t + dt, tps)}, device_id_type=MESH
        )

    @pl.when(z > 0)
    def _():
        pl.semaphore_signal(barrier, inc=1, device_id={"ctx": c - NX}, device_id_type=MESH)

    @pl.when(z < NZ - 1)
    def _():
        pl.semaphore_signal(barrier, inc=1, device_id={"ctx": c + NX}, device_id_type=MESH)

    neighbours = jnp.where((z > 0) & (z < NZ - 1), 2, 1)
    pl.semaphore_wait(barrier, NX - 1 + tps - 1 + neighbours)

    streams = ((kvb, kvw, True), (qb, qbw, False), (gown, gw, False))

    def row_copy(n, dx):
        own, window, _ = streams[n]
        peer = z * NX + lax.rem(x + NX - dx, NX)
        return remote(own, window.at[0, dx], send.at[n, 0, dx], recv.at[n, 0, dx], "ctx", peer)

    def hop_copy(n, s, dx):
        own, window, up = streams[n]
        sems = send.at[n, s, dx], recv.at[n, s, dx], "ctx"
        if dx == TURN:
            peer = z * NX + lax.rem(x + NX - dx, NX)
            return remote(window.at[s, 0], window.at[s, dx], *sems, peer)
        source = own if (s == 1 and dx == 0) else window.at[s - 1, dx]
        peer = jnp.clip(c + NX if up else c - NX, 0, NX * NZ - 1)
        return remote(source, window.at[s, dx], *sems, peer)

    def edge(n, dx, place):
        if streams[n][2]:
            return place + dx < NX
        return (place + dx >= NX) if dx else (place >= 0)

    def sends(n, s, dx):
        up = streams[n][2]
        if dx == TURN:
            cond = (z >= s) if up else (z + s < NZ)
            target = lax.rem(x + NX - dx, NX)
        else:
            cond = ((z >= s - 1) & (z < NZ - 1)) if up else ((z + (s - 1) < NZ) & (z > 0))
            target = x
        return cond & edge(n, dx, target) if s == NX else cond

    def receives(n, s, dx):
        cond = (z >= s) if streams[n][2] else (z + s < NZ)
        return cond & edge(n, dx, x) if s == NX else cond

    def wait_arrival(n, s, dx):
        if s == 0:
            if dx:
                row_copy(n, dx).wait_recv()
        else:

            @pl.when(receives(n, s, dx))
            def _():
                hop_copy(n, s, dx).wait_recv()

    def start_rows(n):
        for dx in range(1, NX):
            row_copy(n, dx).start()

    def start_hop(n, s, dx):
        @pl.when(sends(n, s, dx))
        def _():
            hop_copy(n, s, dx).start()

    def hop(n, s):
        for dx in range(NX):
            if dx != TURN:
                wait_arrival(n, s - 1, dx)
                start_hop(n, s, dx)
                if dx == 0 and s > 1:
                    start_hop(n, s - 1, TURN)

    def cot_copy(dt):
        peer = lax.rem(t + tps - dt, tps)
        return remote(og, cot.at[t], cot_send.at[dt], cot_recv.at[dt], "tp", peer)

    def cot_arrival(dt):
        peer = lax.rem(t + dt, tps)
        return remote(og, cot.at[peer], cot_send.at[dt], cot_recv.at[dt], "tp", peer)

    for dt in range(1, tps):
        cot_copy(dt).start()
    start_rows(0)
    start_rows(1)
    own_kv = pltpu.make_async_copy(kvb, kvw.at[0, 0], local.at[1])
    own_kv.start()
    own_q = pltpu.make_async_copy(qb, qbw.at[0, 0], local.at[2])
    own_q.start()
    cot[t] = og[...]
    hop(0, 1)
    hop(1, 1)
    hop(1, 2)
    for dt in range(1, tps):
        cot_arrival(dt).wait_recv()
    wcopy.wait()
    rows = cot.shape[0] * cot.shape[1]
    gown[...] = dot(cot[...].reshape(rows, cot.shape[2]), wv[...], NT).astype(BF16)
    own_g = pltpu.make_async_copy(gown, gw.at[0, 0], local.at[3])
    own_g.start()
    start_rows(2)
    hop(2, 1)
    for s in range(2, NX + 1):
        hop(0, s)
        if s < NX:
            hop(1, s + 1)
        hop(2, s)
    for n in range(3):
        wait_arrival(n, NX, 0)
        start_hop(n, NX, TURN)
    for n in range(3):
        for dx in range(1, NX):
            if dx == TURN:
                for s in range(NX):
                    wait_arrival(n, s, dx)
            wait_arrival(n, NX, dx)
    for dt in range(1, tps):
        cot_copy(dt).wait_send()
    for n in range(3):
        for dx in range(1, NX):
            row_copy(n, dx).wait_send()
        for s in range(1, NX + 1):
            for dx in range(NX):

                @pl.when(sends(n, s, dx))
                def _():
                    hop_copy(n, s, dx).wait_send()

    own_kv.wait()
    own_q.wait()
    own_g.wait()


def head_cols(h):
    return pl.ds(h * HEAD, HEAD)


def band_hits(band_row, rows, shift=None):
    r = lax.broadcasted_iota(jnp.int32, (rows, BLK), 0)
    want = band_row.astype(jnp.int32)
    if shift is None:
        hit = (r & 7) == want
    else:
        hit = r == want + shift
    return hit.astype(F32).astype(BF16)


def query_kernel(
    heads, meta, pen, kvw, qb, band_rows, gw, ext, w_out, out, grad_q, stats, bias, s_buf, m_buf, l_buf, acc, rsum, att
):
    scale = 1.0 / math.sqrt(HEAD)
    steps = (meta[2, 0] + UNROLL - 1) // UNROLL
    m_buf[...] = jnp.full_like(m_buf, -jnp.inf)
    l_buf[...] = jnp.zeros_like(l_buf)
    acc[...] = jnp.zeros_like(acc)
    rsum[...] = jnp.zeros_like(rsum)

    def first(i, carry):
        for j in [i * UNROLL + u for u in range(UNROLL)]:
            s, dx = meta[0, j], meta[1, j]
            hits = band_hits(kvw[s, dx, 2 * BLK : 2 * BLK + 16, 0:BLK].astype(F32)[0:1], 32)
            for h in range(heads):
                k_h = kvw[s, dx, 0:BLK, head_cols(h)]
                score = dot(qb[0:BLK, head_cols(h)], k_h, NT) * scale + dot(ext[h], hits, NN)
                score = score + pen[j]
                s_buf[j, h] = score
                m_buf[h] = jnp.maximum(m_buf[h], score)
        return carry

    lax.fori_loop(0, steps, first, 0)
    for h in range(heads):
        m_buf[h] = jnp.broadcast_to(jnp.max(m_buf[h], axis=1, keepdims=True), (BLK, BLK))

    def second(i, carry):
        for h in range(heads):
            total, mixed = l_buf[h], acc[h]
            for j in [i * UNROLL + u for u in range(UNROLL)]:
                v_h = kvw[meta[0, j], meta[1, j], BLK : 2 * BLK, head_cols(h)]
                expo = jnp.exp(s_buf[j, h] - m_buf[h])
                total = total + expo
                mixed = mixed + dot(expo.astype(BF16), v_h, NN)
            l_buf[h] = total
            acc[h] = mixed
        return carry

    lax.fori_loop(0, steps, second, 0)
    lane = lax.broadcasted_iota(jnp.int32, (BLK, BLK), 1)
    table = jnp.zeros((BLK, BLK), F32)
    for h in range(heads):
        total = jnp.sum(l_buf[h], axis=1, keepdims=True)
        attended = (acc[h] / total).astype(BF16)
        att[:, head_cols(h)] = attended
        lse = m_buf[h] + jnp.log(total)
        g_h = gw[0:BLK, head_cols(h)].astype(F32)
        delta = jnp.sum(g_h * attended.astype(F32), axis=1, keepdims=True)
        m_buf[h] = lse
        l_buf[h] = jnp.broadcast_to(delta, (BLK, BLK))
        table = jnp.where(lane == h, lse, table)
        table = jnp.where(lane == heads + h, l_buf[h], table)
        acc[h] = jnp.zeros((BLK, HEAD), F32)
    stats[...] = jnp.transpose(table)[0:8]
    out[...] = dot(att[...], w_out[...], NN).astype(BF16)

    def third(i, carry):
        bins = rsum[...]
        for h in range(heads):
            grad = acc[h]
            for j in [i * UNROLL + u for u in range(UNROLL)]:
                s, dx = meta[0, j], meta[1, j]
                band_row = kvw[s, dx, 2 * BLK : 2 * BLK + 16, 0:BLK].astype(F32)[0:1]
                k_h = kvw[s, dx, 0:BLK, head_cols(h)]
                v_h = kvw[s, dx, BLK : 2 * BLK, head_cols(h)]
                prob = jnp.exp(s_buf[j, h] - m_buf[h])
                dprob = dot(gw[0:BLK, head_cols(h)], v_h, NT)
                dscore = prob * (dprob - l_buf[h])
                half = dscore.astype(BF16)
                rest = (dscore - half.astype(F32)).astype(BF16)
                grad = grad + dot(half, k_h, NN)
                hits = band_hits(band_row, BLK, 8 * h)
                bins = bins + (dot(half, hits, NT) + dot(rest, hits, NT))
            acc[h] = grad
        rsum[...] = bins
        return carry

    lax.fori_loop(0, steps, third, 0)
    for h in range(heads):
        grad_q[:, head_cols(h)] = (acc[h] * scale).astype(BF16)
    own = band_rows[:, 0:BLK].astype(F32)[0:1].astype(jnp.int32)
    pick = (lax.broadcasted_iota(jnp.int32, (8, BLK), 0) == own).astype(F32)
    bias[...] = dot(pick, rsum[...], NN, lax.Precision.HIGHEST)


def share_kernel(
    heads, veto, partial, stats, bias, k, v, ext, qbw, gw, attn, grad_k, grad_v, total,
    pieces, window, bx, bz, mid, qv, gv, dk, dv,
    p_send, p_recv, s_send, s_recv, b_send, b_recv, local
):
    c = lax.axis_index("ctx")
    t = lax.axis_index("tp")
    d = lax.axis_index("dp")
    x = lax.rem(c, NX)
    z = c // NX
    tps = partial.shape[0]
    count = window.shape[0]
    ring = NX * NZ
    scale = 1.0 / math.sqrt(HEAD)
    q_load = pltpu.make_async_copy(qbw, qv, local.at[1])
    q_load.start()
    g_load = pltpu.make_async_copy(gw, gv, local.at[2])
    g_load.start()
    dk[...] = jnp.zeros_like(dk)
    dv[...] = jnp.zeros_like(dv)
    barrier = pltpu.get_barrier_semaphore()
    for dc in range(1, ring):
        pl.semaphore_signal(
            barrier, inc=1, device_id={"ctx": lax.rem(c + dc, ring)}, device_id_type=MESH
        )
    for dt in range(1, tps):
        pl.semaphore_signal(
            barrier, inc=1, device_id={"tp": lax.rem(t + dt, tps)}, device_id_type=MESH
        )
    for dz in range(NZ):
        far = {"ctx": lax.rem(z + dz, NZ) * NX + x, "dp": 1 - d}
        pl.semaphore_signal(barrier, inc=1, device_id=far, device_id_type=MESH)
    pl.semaphore_wait(barrier, ring - 1 + tps - 1 + NZ)

    def piece_copy(dt):
        peer = lax.rem(t + dt, tps)
        return remote(partial.at[peer], pieces.at[dt], p_send.at[dt], p_recv.at[dt], "tp", peer)

    def stat_copy(j):
        peer = jnp.clip(c - j, 0, ring - 1)
        return remote(stats, window.at[j], s_send.at[j], s_recv.at[j], "ctx", peer)

    def x_copy(dx, slot):
        peer = z * NX + lax.rem(x + dx, NX)
        return remote(bias, bx.at[slot], b_send.at[0, dx], b_recv.at[0, dx], "ctx", peer)

    def z_copy(side, dz, step):
        other = d if side == 0 else 1 - d
        peer = lax.rem(z + NZ + step * dz, NZ) * NX + x
        slot = d * NZ + z if step > 0 else other * NZ + lax.rem(z + NZ - dz, NZ)
        return pltpu.make_async_remote_copy(
            src_ref=mid,
            dst_ref=bz.at[slot],
            send_sem=b_send.at[1 + side, dz],
            recv_sem=b_recv.at[1 + side, dz],
            device_id={"ctx": peer, "dp": other},
            device_id_type=MESH,
        )

    far_pairs = [(side, dz) for side in range(2) for dz in range(NZ) if side or dz]

    for dx in range(1, NX):
        x_copy(dx, x).start()
    for j in range(1, count):

        @pl.when(c >= j)
        def _():
            stat_copy(j).start()

    for dt in range(1, tps):
        piece_copy(dt).start()
    own_piece = pltpu.make_async_copy(partial.at[t], pieces.at[0], local.at[0])
    own_piece.start()
    window[0] = stats[...]
    bx[x] = bias[...]
    for dx in range(1, NX):
        x_copy(dx, lax.rem(x + NX - dx, NX)).wait_recv()
    mid[...] = (bx[0] + bx[1]) + (bx[2] + bx[3])
    for side, dz in far_pairs:
        z_copy(side, dz, 1).start()
    bz[d * NZ + z] = mid[...]
    for j in range(1, count):

        @pl.when(c + j < ring)
        def _():
            stat_copy(j).wait_recv()

    q_load.wait()
    g_load.wait()

    def step(i, carry):
        for h in range(heads):
            k_h = k[:, head_cols(h)]
            v_h = v[:, head_cols(h)]
            sum_k, sum_v = dk[h], dv[h]
            for j in [i * UNROLL + u for u in range(UNROLL)]:
                there = c + j < jnp.minimum(c + count, ring)
                s = jnp.where(there, (x + j) // NX, 0)
                dx = jnp.where(there, lax.rem(j, NX), 0)
                rows = window[jnp.where(there, j, 0)]
                hits = band_hits(qv[s, dx, BLK : BLK + 16, 0:BLK].astype(F32)[0:1], 32)
                q_h = qv[s, dx, 0:BLK, head_cols(h)]
                g_h = gv[s, dx, :, head_cols(h)]
                score = dot(k_h, q_h, NT) * scale + dot(ext[h], hits, NN)
                prob = jnp.exp(score - (rows[h : h + 1] + veto[j]))
                dprob = dot(v_h, g_h, NT)
                dscore = prob * (dprob - rows[heads + h : heads + h + 1])
                sum_k = sum_k + dot(dscore.astype(BF16), q_h, NN)
                sum_v = sum_v + dot(prob.astype(BF16), g_h, NN)
            dk[h] = sum_k
            dv[h] = sum_v
        return carry

    lax.fori_loop(0, veto.shape[0] // UNROLL, step, 0)
    for h in range(heads):
        grad_k[:, head_cols(h)] = (dk[h] * scale).astype(BF16)
        grad_v[:, head_cols(h)] = dv[h].astype(BF16)
    own_piece.wait()
    for dt in range(1, tps):
        piece_copy(dt).wait_recv()
    out = pieces[0].astype(F32)
    for i in range(1, tps):
        out = out + pieces[i].astype(F32)
    attn[...] = out.astype(BF16)
    for side, dz in far_pairs:
        z_copy(side, dz, -1).wait_recv()
    bins = bz[0]
    for i in range(1, 2 * NZ):
        bins = bins + bz[i]
    total[...] = bins
    for dx in range(1, NX):
        x_copy(dx, x).wait_send()
    for side, dz in far_pairs:
        z_copy(side, dz, 1).wait_send()
    for j in range(1, count):

        @pl.when(c >= j)
        def _():
            stat_copy(j).wait_send()

    for dt in range(1, tps):
        piece_copy(dt).wait_send()


def write_kernel(a, b, c, a_out, b_out, c_out):
    a_out[...] = a[...]
    b_out[...] = b[...]
    c_out[...] = c[...]


def split_bands(values):
    parts = []
    rest = values
    for _ in range(3):
        part = lax.reduce_precision(rest, 8, 7)
        parts.append(part)
        rest = rest - part
    stacked = jnp.stack(parts, axis=2)
    stacked = jnp.pad(stacked, ((0, 0), (0, 0), (0, 1), (0, 8 - values.shape[2])))
    return stacked.reshape(values.shape[0], values.shape[1], 32).astype(BF16)


def body(query, key, value, w_out, output_gradient, key_blocks, band_ids, band_bias):
    q_rows, k_rows, v_rows, og = query[0], key[0], value[0], output_gradient[0]
    bands, lists = band_ids[0], key_blocks[0]
    rows, feats = q_rows.shape
    heads = band_bias.shape[0]
    nblk, window = lists.shape
    width = og.shape[1]
    tps = lax.axis_size("tp")
    c = lax.axis_index("ctx")
    band_rows = jnp.pad(bands.astype(BF16)[None, :], ((0, 15), (0, feats - rows)))
    one_hot = (bands[:, None] == jnp.arange(band_bias.shape[1], dtype=jnp.int32)).astype(F32)
    high = lax.Precision.HIGHEST
    ext_q = split_bands(jnp.einsum("ia,hab->hib", one_hot, band_bias, precision=high))
    ext_k = split_bands(jnp.einsum("kb,hab->hka", one_hot, band_bias, precision=high))
    steps = jnp.arange(window, dtype=jnp.int32)
    queries = c + steps
    own_list = lax.dynamic_index_in_dim(lists, c, 0, keepdims=False)
    later = lax.dynamic_slice_in_dim(
        jnp.pad(lists, ((0, window), (0, 0)), constant_values=-1), c, window, 0
    )
    allow_k = jnp.any(later == c, axis=1) & (queries < nblk)
    extra = -window % UNROLL
    listed = jnp.pad(own_list, (0, extra), constant_values=-1)
    named = listed >= 0
    ids = jnp.where(named, listed, c)
    table = jnp.stack(
        [
            c // NX - ids // NX,
            lax.rem(ids % NX + NX - c % NX, NX),
            jnp.broadcast_to(jnp.sum(named.astype(jnp.int32)), ids.shape),
        ]
    )
    pen = jnp.where(named, 0.0, -1e30).astype(F32)
    veto = jnp.pad(jnp.where(allow_k, 0.0, 1e30).astype(F32), (0, extra), constant_values=1e30)

    vmem = pl.BlockSpec(memory_space=pltpu.VMEM)
    smem = pl.BlockSpec(memory_space=pltpu.SMEM)
    hbm = pl.BlockSpec(memory_space=pl.ANY)
    shape = jax.ShapeDtypeStruct
    kv_shape = (2 * rows + 16, feats)
    qb_shape = (rows + 16, feats)
    kvw, qbw, gw, grad_att = pl.pallas_call(
        exchange_kernel,
        out_shape=(
            shape((NX + 1, NX) + kv_shape, BF16),
            shape((NX + 1, NX) + qb_shape, BF16),
            shape((NX + 1, NX, rows, feats), BF16),
            shape((rows, feats), BF16),
        ),
        in_specs=[vmem] * 5 + [hbm],
        out_specs=(hbm, hbm, hbm, vmem),
        scratch_shapes=[
            pltpu.VMEM(kv_shape, BF16),
            pltpu.VMEM(qb_shape, BF16),
            pltpu.VMEM((tps,) + og.shape, BF16),
            pltpu.VMEM(w_out.shape, BF16),
            pltpu.SemaphoreType.DMA((3, NX + 1, NX)),
            pltpu.SemaphoreType.DMA((3, NX + 1, NX)),
            pltpu.SemaphoreType.DMA((tps,)),
            pltpu.SemaphoreType.DMA((tps,)),
            pltpu.SemaphoreType.DMA((4,)),
        ],
        compiler_params=pltpu.CompilerParams(collective_id=0, has_side_effects=True),
        name="exchange",
    )(q_rows, k_rows, v_rows, band_rows, og, w_out)

    square = pltpu.VMEM((heads, BLK, BLK), F32)
    partial, grad_q, stats, bias = pl.pallas_call(
        functools.partial(query_kernel, heads),
        out_shape=(
            shape((rows, width), BF16),
            shape((rows, feats), BF16),
            shape((8, BLK), F32),
            shape((8, BLK), F32),
        ),
        in_specs=[smem] * 2 + [vmem] * 6,
        out_specs=(vmem,) * 4,
        scratch_shapes=[
            pltpu.VMEM((window + extra, heads, BLK, BLK), F32),
            square,
            square,
            square,
            pltpu.VMEM((BLK, BLK), F32),
            pltpu.VMEM((rows, feats), BF16),
        ],
        name="query_side",
    )(table, pen, kvw, q_rows, band_rows, grad_att, ext_q, w_out)

    tile = (8, BLK)
    attn_out, grad_k, grad_v, bias_total = pl.pallas_call(
        functools.partial(share_kernel, heads),
        out_shape=(
            shape(og.shape, BF16),
            shape((rows, feats), BF16),
            shape((rows, feats), BF16),
            shape(tile, F32),
        ),
        in_specs=[smem] + [vmem] * 6 + [hbm] * 2,
        out_specs=(vmem,) * 4,
        scratch_shapes=[
            pltpu.VMEM((tps,) + og.shape, BF16),
            pltpu.VMEM((window,) + tile, F32),
            pltpu.VMEM((NX,) + tile, F32),
            pltpu.VMEM((2 * NZ,) + tile, F32),
            pltpu.VMEM(tile, F32),
            pltpu.VMEM(qbw.shape, BF16),
            pltpu.VMEM(gw.shape, BF16),
            square,
            square,
            pltpu.SemaphoreType.DMA((tps,)),
            pltpu.SemaphoreType.DMA((tps,)),
            pltpu.SemaphoreType.DMA((window,)),
            pltpu.SemaphoreType.DMA((window,)),
            pltpu.SemaphoreType.DMA((3, NZ)),
            pltpu.SemaphoreType.DMA((3, NZ)),
            pltpu.SemaphoreType.DMA((3,)),
        ],
        compiler_params=pltpu.CompilerParams(collective_id=1, has_side_effects=True),
        name="share",
    )(
        veto, partial.reshape((tps,) + og.shape), stats, bias,
        k_rows, v_rows, ext_k, qbw, gw,
    )

    attn_out, grad_k, grad_v = pl.pallas_call(
        write_kernel,
        out_shape=(shape(og.shape, BF16), shape((rows, feats), BF16), shape((rows, feats), BF16)),
        in_specs=[vmem] * 3,
        out_specs=(vmem,) * 3,
        name="write_out",
    )(attn_out, grad_k, grad_v)

    na, nb = band_bias.shape[1:]
    grad_bias = bias_total[:na, : 8 * heads].reshape(na, heads, 8)[:, :, :nb].transpose(1, 0, 2)
    return (attn_out[None], grad_q[None], grad_k[None], grad_v[None], grad_bias)


def solution(mesh):
    return jax.shard_map(
        body,
        mesh=mesh,
        in_specs=(
            P("dp", "ctx", "tp"),
            P("dp", "ctx", "tp"),
            P("dp", "ctx", "tp"),
            P("tp", None),
            P("dp", ("ctx", "tp"), None),
            P("dp", None, None),
            P("dp", "ctx"),
            P("tp", None, None),
        ),
        out_specs=(
            P("dp", ("ctx", "tp"), None),
            P("dp", "ctx", "tp"),
            P("dp", "ctx", "tp"),
            P("dp", "ctx", "tp"),
            P("tp", None, None),
        ),
        check_vma=False,
    )
```

```python
import functools
import math

import jax
import jax.numpy as jnp
from jax import lax
from jax.experimental import pallas as pl
from jax.experimental.pallas import tpu as pltpu
from jax.sharding import PartitionSpec as P

HEAD = 128
BLK = 128
NX = 4
NZ = 8
TURN = 3
UNROLL = 3
MESH = pl.DeviceIdType.MESH
F32 = jnp.float32
BF16 = jnp.bfloat16
NT = (((1,), (1,)), ((), ()))
NN = (((1,), (0,)), ((), ()))


def dot(a, b, dims, precision=None):
    return lax.dot_general(a, b, dims, preferred_element_type=F32, precision=precision)


def remote(src, dst, send, recv, axis, index):
    return pltpu.make_async_remote_copy(
        src_ref=src,
        dst_ref=dst,
        send_sem=send,
        recv_sem=recv,
        device_id={axis: index},
        device_id_type=MESH,
    )


def exchange_kernel(
    q, k, v, bands, og, w_hbm, kvw, qbw, gw, gown, kvb, qb, cot, wv,
    send, recv, cot_send, cot_recv, local
):
    c = lax.axis_index("ctx")
    t = lax.axis_index("tp")
    x = lax.rem(c, NX)
    z = c // NX
    tps = cot.shape[0]
    wcopy = pltpu.make_async_copy(w_hbm, wv, local.at[0])
    wcopy.start()
    kvb[0:BLK] = k[...]
    kvb[BLK : 2 * BLK] = v[...]
    qb[0:BLK] = q[...]
    tail = jnp.broadcast_to(bands[...].astype(F32), (16, BLK)).astype(BF16)
    kvb[2 * BLK :] = jnp.zeros((16, kvb.shape[1]), BF16)
    kvb[2 * BLK :, 0:BLK] = tail
    qb[BLK:] = jnp.zeros((16, qb.shape[1]), BF16)
    qb[BLK:, 0:BLK] = tail

    barrier = pltpu.get_barrier_semaphore()
    for dx in range(1, NX):
        peer = z * NX + lax.rem(x + dx, NX)
        pl.semaphore_signal(barrier, inc=1, device_id={"ctx": peer}, device_id_type=MESH)
    for dt in range(1, tps):
        pl.semaphore_signal(
            barrier, inc=1, device_id={"tp": lax.rem(t + dt, tps)}, device_id_type=MESH
        )

    @pl.when(z > 0)
    def _():
        pl.semaphore_signal(barrier, inc=1, device_id={"ctx": c - NX}, device_id_type=MESH)

    @pl.when(z < NZ - 1)
    def _():
        pl.semaphore_signal(barrier, inc=1, device_id={"ctx": c + NX}, device_id_type=MESH)

    neighbours = jnp.where((z > 0) & (z < NZ - 1), 2, 1)
    pl.semaphore_wait(barrier, NX - 1 + tps - 1 + neighbours)

    streams = ((kvb, kvw, True), (qb, qbw, False), (gown, gw, False))

    def row_copy(n, dx):
        own, window, _ = streams[n]
        peer = z * NX + lax.rem(x + NX - dx, NX)
        return remote(own, window.at[0, dx], send.at[n, 0, dx], recv.at[n, 0, dx], "ctx", peer)

    def hop_copy(n, s, dx):
        own, window, up = streams[n]
        sems = send.at[n, s, dx], recv.at[n, s, dx], "ctx"
        if dx == TURN:
            peer = z * NX + lax.rem(x + NX - dx, NX)
            return remote(window.at[s, 0], window.at[s, dx], *sems, peer)
        source = own if (s == 1 and dx == 0) else window.at[s - 1, dx]
        peer = jnp.clip(c + NX if up else c - NX, 0, NX * NZ - 1)
        return remote(source, window.at[s, dx], *sems, peer)

    def edge(n, dx, place):
        if streams[n][2]:
            return place + dx < NX
        return (place + dx >= NX) if dx else (place >= 0)

    def sends(n, s, dx):
        up = streams[n][2]
        if dx == TURN:
            cond = (z >= s) if up else (z + s < NZ)
            target = lax.rem(x + NX - dx, NX)
        else:
            cond = ((z >= s - 1) & (z < NZ - 1)) if up else ((z + (s - 1) < NZ) & (z > 0))
            target = x
        return cond & edge(n, dx, target) if s == NX else cond

    def receives(n, s, dx):
        cond = (z >= s) if streams[n][2] else (z + s < NZ)
        return cond & edge(n, dx, x) if s == NX else cond

    def wait_arrival(n, s, dx):
        if s == 0:
            if dx:
                row_copy(n, dx).wait_recv()
        else:

            @pl.when(receives(n, s, dx))
            def _():
                hop_copy(n, s, dx).wait_recv()

    def start_rows(n):
        for dx in range(1, NX):
            row_copy(n, dx).start()

    def start_hop(n, s, dx):
        @pl.when(sends(n, s, dx))
        def _():
            hop_copy(n, s, dx).start()

    def hop(n, s):
        for dx in range(NX):
            if dx != TURN:
                wait_arrival(n, s - 1, dx)
                start_hop(n, s, dx)
                if dx == 0 and s > 1:
                    start_hop(n, s - 1, TURN)

    def cot_copy(dt):
        peer = lax.rem(t + tps - dt, tps)
        return remote(og, cot.at[t], cot_send.at[dt], cot_recv.at[dt], "tp", peer)

    def cot_arrival(dt):
        peer = lax.rem(t + dt, tps)
        return remote(og, cot.at[peer], cot_send.at[dt], cot_recv.at[dt], "tp", peer)

    for dt in range(1, tps):
        cot_copy(dt).start()
    start_rows(0)
    start_rows(1)
    own_kv = pltpu.make_async_copy(kvb, kvw.at[0, 0], local.at[1])
    own_kv.start()
    own_q = pltpu.make_async_copy(qb, qbw.at[0, 0], local.at[2])
    own_q.start()
    cot[t] = og[...]
    hop(0, 1)
    hop(1, 1)
    hop(1, 2)
    for dt in range(1, tps):
        cot_arrival(dt).wait_recv()
    wcopy.wait()
    rows = cot.shape[0] * cot.shape[1]
    gown[...] = dot(cot[...].reshape(rows, cot.shape[2]), wv[...], NT).astype(BF16)
    own_g = pltpu.make_async_copy(gown, gw.at[0, 0], local.at[3])
    own_g.start()
    start_rows(2)
    hop(2, 1)
    for s in range(2, NX + 1):
        hop(0, s)
        if s < NX:
            hop(1, s + 1)
        hop(2, s)
    for n in range(3):
        wait_arrival(n, NX, 0)
        start_hop(n, NX, TURN)
    for n in range(3):
        for dx in range(1, NX):
            if dx == TURN:
                for s in range(NX):
                    wait_arrival(n, s, dx)
            wait_arrival(n, NX, dx)
    for dt in range(1, tps):
        cot_copy(dt).wait_send()
    for n in range(3):
        for dx in range(1, NX):
            row_copy(n, dx).wait_send()
        for s in range(1, NX + 1):
            for dx in range(NX):

                @pl.when(sends(n, s, dx))
                def _():
                    hop_copy(n, s, dx).wait_send()

    own_kv.wait()
    own_q.wait()
    own_g.wait()


def head_cols(h):
    return pl.ds(h * HEAD, HEAD)


def band_hits(band_row, rows, shift=None):
    r = lax.broadcasted_iota(jnp.int32, (rows, BLK), 0)
    want = band_row.astype(jnp.int32)
    if shift is None:
        hit = (r & 7) == want
    else:
        hit = r == want + shift
    return hit.astype(F32).astype(BF16)


def query_kernel(
    heads, lists, kvw, qb, bands, gw, ext, w_out, out, grad_q, stats, bias, veto, s_buf, m_buf, l_buf, acc, rsum, att
):
    scale = 1.0 / math.sqrt(HEAD)
    c = lax.axis_index("ctx")
    nblk, window = lists.shape
    named = lax.fori_loop(
        0, window, lambda j, n: n + (lists[c, j] >= 0).astype(jnp.int32), jnp.int32(0)
    )
    steps = (named + UNROLL - 1) // UNROLL

    def entry(j):
        found = lists[c, jnp.minimum(j, window - 1)]
        valid = (j < window) & (found >= 0)
        block = jnp.where(valid, found, c)
        dx = lax.rem(lax.rem(block, NX) + NX - lax.rem(c, NX), NX)
        return c // NX - block // NX, dx, jnp.where(valid, 0.0, -1e30)

    def judge(j, carry):
        later = jnp.minimum(c + j, nblk - 1)
        hit = lists[later, 0] == c
        for m in range(1, window):
            hit = hit | (lists[later, m] == c)
        hit = hit & (j < window) & (c + j < nblk)
        veto[j] = jnp.where(hit, 0.0, 1e30)
        return carry

    lax.fori_loop(0, veto.shape[0], judge, 0)
    m_buf[...] = jnp.full_like(m_buf, -jnp.inf)
    l_buf[...] = jnp.zeros_like(l_buf)
    acc[...] = jnp.zeros_like(acc)
    rsum[...] = jnp.zeros_like(rsum)

    def first(i, carry):
        for j in [i * UNROLL + u for u in range(UNROLL)]:
            s, dx, pen = entry(j)
            hits = band_hits(kvw[s, dx, 2 * BLK : 2 * BLK + 16, 0:BLK].astype(F32)[0:1], 32)
            for h in range(heads):
                k_h = kvw[s, dx, 0:BLK, head_cols(h)]
                score = dot(qb[0:BLK, head_cols(h)], k_h, NT) * scale + dot(ext[h], hits, NN)
                score = score + pen
                s_buf[j, h] = score
                m_buf[h] = jnp.maximum(m_buf[h], score)
        return carry

    lax.fori_loop(0, steps, first, 0)
    for h in range(heads):
        m_buf[h] = jnp.broadcast_to(jnp.max(m_buf[h], axis=1, keepdims=True), (BLK, BLK))

    def second(i, carry):
        for h in range(heads):
            total, mixed = l_buf[h], acc[h]
            for j in [i * UNROLL + u for u in range(UNROLL)]:
                s, dx, _ = entry(j)
                v_h = kvw[s, dx, BLK : 2 * BLK, head_cols(h)]
                expo = jnp.exp(s_buf[j, h] - m_buf[h])
                total = total + expo
                mixed = mixed + dot(expo.astype(BF16), v_h, NN)
            l_buf[h] = total
            acc[h] = mixed
        return carry

    lax.fori_loop(0, steps, second, 0)
    lane = lax.broadcasted_iota(jnp.int32, (BLK, BLK), 1)
    table = jnp.zeros((BLK, BLK), F32)
    for h in range(heads):
        total = jnp.sum(l_buf[h], axis=1, keepdims=True)
        attended = (acc[h] / total).astype(BF16)
        att[:, head_cols(h)] = attended
        lse = m_buf[h] + jnp.log(total)
        g_h = gw[0:BLK, head_cols(h)].astype(F32)
        delta = jnp.sum(g_h * attended.astype(F32), axis=1, keepdims=True)
        m_buf[h] = lse
        l_buf[h] = jnp.broadcast_to(delta, (BLK, BLK))
        table = jnp.where(lane == h, lse, table)
        table = jnp.where(lane == heads + h, l_buf[h], table)
        acc[h] = jnp.zeros((BLK, HEAD), F32)
    stats[...] = jnp.transpose(table)[0:8]
    out[...] = dot(att[...], w_out[...], NN).astype(BF16)

    def third(i, carry):
        bins = rsum[...]
        for h in range(heads):
            grad = acc[h]
            for j in [i * UNROLL + u for u in range(UNROLL)]:
                s, dx, _ = entry(j)
                band_row = kvw[s, dx, 2 * BLK : 2 * BLK + 16, 0:BLK].astype(F32)[0:1]
                k_h = kvw[s, dx, 0:BLK, head_cols(h)]
                v_h = kvw[s, dx, BLK : 2 * BLK, head_cols(h)]
                prob = jnp.exp(s_buf[j, h] - m_buf[h])
                dprob = dot(gw[0:BLK, head_cols(h)], v_h, NT)
                dscore = prob * (dprob - l_buf[h])
                half = dscore.astype(BF16)
                rest = (dscore - half.astype(F32)).astype(BF16)
                grad = grad + dot(half, k_h, NN)
                hits = band_hits(band_row, BLK, 8 * h)
                bins = bins + (dot(half, hits, NT) + dot(rest, hits, NT))
            acc[h] = grad
        rsum[...] = bins
        return carry

    lax.fori_loop(0, steps, third, 0)
    for h in range(heads):
        grad_q[:, head_cols(h)] = (acc[h] * scale).astype(BF16)
    own = bands[...]
    pick = (lax.broadcasted_iota(jnp.int32, (8, BLK), 0) == own).astype(F32)
    bias[...] = dot(pick, rsum[...], NN, lax.Precision.HIGHEST)


def share_kernel(
    heads, veto, partial, stats, bias, k, v, ext, qbw, gw, attn, grad_k, grad_v, total,
    pieces, window, bx, bz, mid, qv, gv, dk, dv,
    p_send, p_recv, s_send, s_recv, b_send, b_recv, local
):
    c = lax.axis_index("ctx")
    t = lax.axis_index("tp")
    d = lax.axis_index("dp")
    x = lax.rem(c, NX)
    z = c // NX
    tps = partial.shape[0]
    count = window.shape[0]
    ring = NX * NZ
    scale = 1.0 / math.sqrt(HEAD)
    q_load = pltpu.make_async_copy(qbw, qv, local.at[1])
    q_load.start()
    g_load = pltpu.make_async_copy(gw, gv, local.at[2])
    g_load.start()
    dk[...] = jnp.zeros_like(dk)
    dv[...] = jnp.zeros_like(dv)
    barrier = pltpu.get_barrier_semaphore()
    for dc in range(1, ring):
        pl.semaphore_signal(
            barrier, inc=1, device_id={"ctx": lax.rem(c + dc, ring)}, device_id_type=MESH
        )
    for dt in range(1, tps):
        pl.semaphore_signal(
            barrier, inc=1, device_id={"tp": lax.rem(t + dt, tps)}, device_id_type=MESH
        )
    for dz in range(NZ):
        far = {"ctx": lax.rem(z + dz, NZ) * NX + x, "dp": 1 - d}
        pl.semaphore_signal(barrier, inc=1, device_id=far, device_id_type=MESH)
    pl.semaphore_wait(barrier, ring - 1 + tps - 1 + NZ)

    def piece_copy(dt):
        peer = lax.rem(t + dt, tps)
        return remote(partial.at[peer], pieces.at[dt], p_send.at[dt], p_recv.at[dt], "tp", peer)

    def stat_copy(j):
        peer = jnp.clip(c - j, 0, ring - 1)
        return remote(stats, window.at[j], s_send.at[j], s_recv.at[j], "ctx", peer)

    def x_copy(dx, slot):
        peer = z * NX + lax.rem(x + dx, NX)
        return remote(bias, bx.at[slot], b_send.at[0, dx], b_recv.at[0, dx], "ctx", peer)

    def z_copy(side, dz, step):
        other = d if side == 0 else 1 - d
        peer = lax.rem(z + NZ + step * dz, NZ) * NX + x
        slot = d * NZ + z if step > 0 else other * NZ + lax.rem(z + NZ - dz, NZ)
        return pltpu.make_async_remote_copy(
            src_ref=mid,
            dst_ref=bz.at[slot],
            send_sem=b_send.at[1 + side, dz],
            recv_sem=b_recv.at[1 + side, dz],
            device_id={"ctx": peer, "dp": other},
            device_id_type=MESH,
        )

    far_pairs = [(side, dz) for side in range(2) for dz in range(NZ) if side or dz]

    for dx in range(1, NX):
        x_copy(dx, x).start()
    for j in range(1, count):

        @pl.when(c >= j)
        def _():
            stat_copy(j).start()

    for dt in range(1, tps):
        piece_copy(dt).start()
    own_piece = pltpu.make_async_copy(partial.at[t], pieces.at[0], local.at[0])
    own_piece.start()
    window[0] = stats[...]
    bx[x] = bias[...]
    for dx in range(1, NX):
        x_copy(dx, lax.rem(x + NX - dx, NX)).wait_recv()
    mid[...] = (bx[0] + bx[1]) + (bx[2] + bx[3])
    for side, dz in far_pairs:
        z_copy(side, dz, 1).start()
    bz[d * NZ + z] = mid[...]
    for j in range(1, count):

        @pl.when(c + j < ring)
        def _():
            stat_copy(j).wait_recv()

    q_load.wait()
    g_load.wait()

    def step(i, carry):
        for h in range(heads):
            k_h = k[:, head_cols(h)]
            v_h = v[:, head_cols(h)]
            sum_k, sum_v = dk[h], dv[h]
            for j in [i * UNROLL + u for u in range(UNROLL)]:
                there = c + j < jnp.minimum(c + count, ring)
                s = jnp.where(there, (x + j) // NX, 0)
                dx = jnp.where(there, lax.rem(j, NX), 0)
                rows = window[jnp.where(there, j, 0)]
                hits = band_hits(qv[s, dx, BLK : BLK + 16, 0:BLK].astype(F32)[0:1], 32)
                q_h = qv[s, dx, 0:BLK, head_cols(h)]
                g_h = gv[s, dx, :, head_cols(h)]
                score = dot(k_h, q_h, NT) * scale + dot(ext[h], hits, NN)
                prob = jnp.exp(score - (rows[h : h + 1] + veto[j]))
                dprob = dot(v_h, g_h, NT)
                dscore = prob * (dprob - rows[heads + h : heads + h + 1])
                sum_k = sum_k + dot(dscore.astype(BF16), q_h, NN)
                sum_v = sum_v + dot(prob.astype(BF16), g_h, NN)
            dk[h] = sum_k
            dv[h] = sum_v
        return carry

    lax.fori_loop(0, veto.shape[0] // UNROLL, step, 0)
    for h in range(heads):
        grad_k[:, head_cols(h)] = (dk[h] * scale).astype(BF16)
        grad_v[:, head_cols(h)] = dv[h].astype(BF16)
    own_piece.wait()
    for dt in range(1, tps):
        piece_copy(dt).wait_recv()
    out = pieces[0].astype(F32)
    for i in range(1, tps):
        out = out + pieces[i].astype(F32)
    attn[...] = out.astype(BF16)
    for side, dz in far_pairs:
        z_copy(side, dz, -1).wait_recv()
    bins = bz[0]
    for i in range(1, 2 * NZ):
        bins = bins + bz[i]
    total[...] = bins
    for dx in range(1, NX):
        x_copy(dx, x).wait_send()
    for side, dz in far_pairs:
        z_copy(side, dz, 1).wait_send()
    for j in range(1, count):

        @pl.when(c >= j)
        def _():
            stat_copy(j).wait_send()

    for dt in range(1, tps):
        piece_copy(dt).wait_send()


def write_kernel(a, b, c, a_out, b_out, c_out):
    a_out[...] = a[...]
    b_out[...] = b[...]
    c_out[...] = c[...]


def split_bands(values):
    parts = []
    rest = values
    for _ in range(3):
        part = lax.reduce_precision(rest, 8, 7)
        parts.append(part)
        rest = rest - part
    stacked = jnp.stack(parts, axis=2)
    stacked = jnp.pad(stacked, ((0, 0), (0, 0), (0, 1), (0, 8 - values.shape[2])))
    return stacked.reshape(values.shape[0], values.shape[1], 32).astype(BF16)


def body(query, key, value, w_out, output_gradient, key_blocks, band_ids, band_bias):
    q_rows, k_rows, v_rows, og = query[0], key[0], value[0], output_gradient[0]
    bands, lists = band_ids[0], key_blocks[0]
    rows, feats = q_rows.shape
    heads = band_bias.shape[0]
    window = lists.shape[1]
    width = og.shape[1]
    tps = lax.axis_size("tp")
    c = lax.axis_index("ctx")
    band_row = bands[None, :]
    one_hot = (bands[:, None] == jnp.arange(band_bias.shape[1], dtype=jnp.int32)).astype(F32)
    high = lax.Precision.HIGHEST
    ext_q = split_bands(jnp.einsum("ia,hab->hib", one_hot, band_bias, precision=high))
    ext_k = split_bands(jnp.einsum("kb,hab->hka", one_hot, band_bias, precision=high))
    extra = -window % UNROLL

    vmem = pl.BlockSpec(memory_space=pltpu.VMEM)
    smem = pl.BlockSpec(memory_space=pltpu.SMEM)
    hbm = pl.BlockSpec(memory_space=pl.ANY)
    shape = jax.ShapeDtypeStruct
    kv_shape = (2 * rows + 16, feats)
    qb_shape = (rows + 16, feats)
    kvw, qbw, gw, grad_att = pl.pallas_call(
        exchange_kernel,
        out_shape=(
            shape((NX + 1, NX) + kv_shape, BF16),
            shape((NX + 1, NX) + qb_shape, BF16),
            shape((NX + 1, NX, rows, feats), BF16),
            shape((rows, feats), BF16),
        ),
        in_specs=[vmem] * 5 + [hbm],
        out_specs=(hbm, hbm, hbm, vmem),
        scratch_shapes=[
            pltpu.VMEM(kv_shape, BF16),
            pltpu.VMEM(qb_shape, BF16),
            pltpu.VMEM((tps,) + og.shape, BF16),
            pltpu.VMEM(w_out.shape, BF16),
            pltpu.SemaphoreType.DMA((3, NX + 1, NX)),
            pltpu.SemaphoreType.DMA((3, NX + 1, NX)),
            pltpu.SemaphoreType.DMA((tps,)),
            pltpu.SemaphoreType.DMA((tps,)),
            pltpu.SemaphoreType.DMA((4,)),
        ],
        compiler_params=pltpu.CompilerParams(collective_id=0, has_side_effects=True),
        name="exchange",
    )(q_rows, k_rows, v_rows, band_row, og, w_out)

    square = pltpu.VMEM((heads, BLK, BLK), F32)
    partial, grad_q, stats, bias, veto = pl.pallas_call(
        functools.partial(query_kernel, heads),
        out_shape=(
            shape((rows, width), BF16),
            shape((rows, feats), BF16),
            shape((8, BLK), F32),
            shape((8, BLK), F32),
            shape((window + extra,), F32),
        ),
        in_specs=[smem] + [vmem] * 6,
        out_specs=(vmem,) * 4 + (smem,),
        scratch_shapes=[
            pltpu.VMEM((window + extra, heads, BLK, BLK), F32),
            square,
            square,
            square,
            pltpu.VMEM((BLK, BLK), F32),
            pltpu.VMEM((rows, feats), BF16),
        ],
        name="query_side",
    )(lists, kvw, q_rows, band_row, grad_att, ext_q, w_out)

    tile = (8, BLK)
    attn_out, grad_k, grad_v, bias_total = pl.pallas_call(
        functools.partial(share_kernel, heads),
        out_shape=(
            shape(og.shape, BF16),
            shape((rows, feats), BF16),
            shape((rows, feats), BF16),
            shape(tile, F32),
        ),
        in_specs=[smem] + [vmem] * 6 + [hbm] * 2,
        out_specs=(vmem,) * 4,
        scratch_shapes=[
            pltpu.VMEM((tps,) + og.shape, BF16),
            pltpu.VMEM((window,) + tile, F32),
            pltpu.VMEM((NX,) + tile, F32),
            pltpu.VMEM((2 * NZ,) + tile, F32),
            pltpu.VMEM(tile, F32),
            pltpu.VMEM(qbw.shape, BF16),
            pltpu.VMEM(gw.shape, BF16),
            square,
            square,
            pltpu.SemaphoreType.DMA((tps,)),
            pltpu.SemaphoreType.DMA((tps,)),
            pltpu.SemaphoreType.DMA((window,)),
            pltpu.SemaphoreType.DMA((window,)),
            pltpu.SemaphoreType.DMA((3, NZ)),
            pltpu.SemaphoreType.DMA((3, NZ)),
            pltpu.SemaphoreType.DMA((3,)),
        ],
        compiler_params=pltpu.CompilerParams(collective_id=1, has_side_effects=True),
        name="share",
    )(
        veto, partial.reshape((tps,) + og.shape), stats, bias,
        k_rows, v_rows, ext_k, qbw, gw,
    )

    attn_out, grad_k, grad_v = pl.pallas_call(
        write_kernel,
        out_shape=(shape(og.shape, BF16), shape((rows, feats), BF16), shape((rows, feats), BF16)),
        in_specs=[vmem] * 3,
        out_specs=(vmem,) * 3,
        name="write_out",
    )(attn_out, grad_k, grad_v)

    na, nb = band_bias.shape[1:]
    grad_bias = bias_total[:na, : 8 * heads].reshape(na, heads, 8)[:, :, :nb].transpose(1, 0, 2)
    return (attn_out[None], grad_q[None], grad_k[None], grad_v[None], grad_bias)


def solution(mesh):
    return jax.shard_map(
        body,
        mesh=mesh,
        in_specs=(
            P("dp", "ctx", "tp"),
            P("dp", "ctx", "tp"),
            P("dp", "ctx", "tp"),
            P("tp", None),
            P("dp", ("ctx", "tp"), None),
            P("dp", None, None),
            P("dp", "ctx"),
            P("tp", None, None),
        ),
        out_specs=(
            P("dp", ("ctx", "tp"), None),
            P("dp", "ctx", "tp"),
            P("dp", "ctx", "tp"),
            P("dp", "ctx", "tp"),
            P("tp", None, None),
        ),
        check_vma=False,
    )
```

```python
import functools
import math

import jax
import jax.numpy as jnp
from jax import lax
from jax.experimental import pallas as pl
from jax.experimental.pallas import tpu as pltpu
from jax.sharding import PartitionSpec as P

HEAD = 128
BLK = 128
NX = 4
NZ = 8
BOTH = (1, 3)
ONE = (3,)
UNROLL = 3
MESH = pl.DeviceIdType.MESH
F32 = jnp.float32
BF16 = jnp.bfloat16
NT = (((1,), (1,)), ((), ()))
NN = (((1,), (0,)), ((), ()))


def dot(a, b, dims, precision=None):
    return lax.dot_general(a, b, dims, preferred_element_type=F32, precision=precision)


def remote(src, dst, send, recv, axis, index):
    return pltpu.make_async_remote_copy(
        src_ref=src,
        dst_ref=dst,
        send_sem=send,
        recv_sem=recv,
        device_id={axis: index},
        device_id_type=MESH,
    )


def exchange_kernel(
    q, k, v, bands, og, w_hbm, kw, vw, qbw, gw, gown, kb, qb, cot, wv,
    send, recv, cot_send, cot_recv, local
):
    c = lax.axis_index("ctx")
    t = lax.axis_index("tp")
    x = lax.rem(c, NX)
    z = c // NX
    tps = cot.shape[0]
    wcopy = pltpu.make_async_copy(w_hbm, wv, local.at[0])
    wcopy.start()
    kb[0:BLK] = k[...]
    qb[0:BLK] = q[...]
    tail = jnp.broadcast_to(bands[...].astype(F32), (16, BLK)).astype(BF16)
    kb[BLK:] = jnp.zeros((16, kb.shape[1]), BF16)
    kb[BLK:, 0:BLK] = tail
    qb[BLK:] = jnp.zeros((16, qb.shape[1]), BF16)
    qb[BLK:, 0:BLK] = tail

    barrier = pltpu.get_barrier_semaphore()
    for dx in range(1, NX):
        peer = z * NX + lax.rem(x + dx, NX)
        pl.semaphore_signal(barrier, inc=1, device_id={"ctx": peer}, device_id_type=MESH)
    for dt in range(1, tps):
        pl.semaphore_signal(
            barrier, inc=1, device_id={"tp": lax.rem(t + dt, tps)}, device_id_type=MESH
        )

    @pl.when(z > 0)
    def _():
        pl.semaphore_signal(barrier, inc=1, device_id={"ctx": c - NX}, device_id_type=MESH)

    @pl.when(z < NZ - 1)
    def _():
        pl.semaphore_signal(barrier, inc=1, device_id={"ctx": c + NX}, device_id_type=MESH)

    neighbours = jnp.where((z > 0) & (z < NZ - 1), 2, 1)
    pl.semaphore_wait(barrier, NX - 1 + tps - 1 + neighbours)

    streams = (
        (kb, kw, True, BOTH),
        (qb, qbw, False, BOTH),
        (gown, gw, False, ONE),
        (v, vw, True, ONE),
    )

    def row_copy(n, dx):
        own, window = streams[n][:2]
        peer = z * NX + lax.rem(x + NX - dx, NX)
        return remote(own, window.at[0, dx], send.at[n, 0, dx], recv.at[n, 0, dx], "ctx", peer)

    def hop_copy(n, s, dx):
        own, window, up, turns = streams[n]
        sems = send.at[n, s, dx], recv.at[n, s, dx], "ctx"
        if dx in turns:
            peer = z * NX + lax.rem(x + NX - dx, NX)
            return remote(window.at[s, 0], window.at[s, dx], *sems, peer)
        source = own if (s == 1 and dx == 0) else window.at[s - 1, dx]
        peer = jnp.clip(c + NX if up else c - NX, 0, NX * NZ - 1)
        return remote(source, window.at[s, dx], *sems, peer)

    def edge(n, dx, place):
        if streams[n][2]:
            return place + dx < NX
        return (place + dx >= NX) if dx else (place >= 0)

    def sends(n, s, dx):
        up, turns = streams[n][2:]
        if dx in turns:
            cond = (z >= s) if up else (z + s < NZ)
            target = lax.rem(x + NX - dx, NX)
        else:
            cond = ((z >= s - 1) & (z < NZ - 1)) if up else ((z + (s - 1) < NZ) & (z > 0))
            target = x
        return cond & edge(n, dx, target) if s == NX else cond

    def receives(n, s, dx):
        cond = (z >= s) if streams[n][2] else (z + s < NZ)
        return cond & edge(n, dx, x) if s == NX else cond

    def wait_arrival(n, s, dx):
        if s == 0:
            if dx:
                row_copy(n, dx).wait_recv()
        else:

            @pl.when(receives(n, s, dx))
            def _():
                hop_copy(n, s, dx).wait_recv()

    def start_rows(n):
        for dx in range(1, NX):
            row_copy(n, dx).start()

    def start_hop(n, s, dx):
        @pl.when(sends(n, s, dx))
        def _():
            hop_copy(n, s, dx).start()

    def hop(n, s):
        turns = streams[n][3]
        for dx in range(NX):
            if dx not in turns:
                wait_arrival(n, s - 1, dx)
                start_hop(n, s, dx)
                if dx == 0 and s > 1:
                    for turn in turns:
                        start_hop(n, s - 1, turn)

    def cot_copy(dt):
        peer = lax.rem(t + tps - dt, tps)
        return remote(og, cot.at[t], cot_send.at[dt], cot_recv.at[dt], "tp", peer)

    def cot_arrival(dt):
        peer = lax.rem(t + dt, tps)
        return remote(og, cot.at[peer], cot_send.at[dt], cot_recv.at[dt], "tp", peer)

    for dt in range(1, tps):
        cot_copy(dt).start()
    start_rows(0)
    start_rows(3)
    start_rows(1)
    own_k = pltpu.make_async_copy(kb, kw.at[0, 0], local.at[1])
    own_k.start()
    own_v = pltpu.make_async_copy(v, vw.at[0, 0], local.at[4])
    own_v.start()
    own_q = pltpu.make_async_copy(qb, qbw.at[0, 0], local.at[2])
    own_q.start()
    cot[t] = og[...]
    hop(0, 1)
    hop(3, 1)
    hop(1, 1)
    hop(1, 2)
    for dt in range(1, tps):
        cot_arrival(dt).wait_recv()
    wcopy.wait()
    rows = cot.shape[0] * cot.shape[1]
    gown[...] = dot(cot[...].reshape(rows, cot.shape[2]), wv[...], NT).astype(BF16)
    own_g = pltpu.make_async_copy(gown, gw.at[0, 0], local.at[3])
    own_g.start()
    start_rows(2)
    hop(2, 1)
    for s in range(2, NX + 1):
        hop(0, s)
        hop(3, s)
        if s < NX:
            hop(1, s + 1)
        hop(2, s)
    for n in range(len(streams)):
        wait_arrival(n, NX, 0)
        for turn in streams[n][3]:
            start_hop(n, NX, turn)
    for n in range(len(streams)):
        for dx in range(1, NX):
            if dx in streams[n][3]:
                for s in range(NX):
                    wait_arrival(n, s, dx)
            wait_arrival(n, NX, dx)
    for dt in range(1, tps):
        cot_copy(dt).wait_send()
    for n in range(len(streams)):
        for dx in range(1, NX):
            row_copy(n, dx).wait_send()
        for s in range(1, NX + 1):
            for dx in range(NX):

                @pl.when(sends(n, s, dx))
                def _():
                    hop_copy(n, s, dx).wait_send()

    own_k.wait()
    own_v.wait()
    own_q.wait()
    own_g.wait()


def head_cols(h):
    return pl.ds(h * HEAD, HEAD)


def band_hits(band_row, rows, shift=None):
    r = lax.broadcasted_iota(jnp.int32, (rows, BLK), 0)
    want = band_row.astype(jnp.int32)
    if shift is None:
        hit = (r & 7) == want
    else:
        hit = r == want + shift
    return hit.astype(F32).astype(BF16)


def query_kernel(
    heads, lists, kw, vw, qb, bands, gw, ext, w_out, out, grad_q, stats, bias, veto, s_buf, m_buf, l_buf, acc, rsum, att
):
    scale = 1.0 / math.sqrt(HEAD)
    c = lax.axis_index("ctx")
    nblk, window = lists.shape
    named = lax.fori_loop(
        0, window, lambda j, n: n + (lists[c, j] >= 0).astype(jnp.int32), jnp.int32(0)
    )
    steps = (named + UNROLL - 1) // UNROLL

    def entry(j):
        found = lists[c, jnp.minimum(j, window - 1)]
        valid = (j < window) & (found >= 0)
        block = jnp.where(valid, found, c)
        dx = lax.rem(lax.rem(block, NX) + NX - lax.rem(c, NX), NX)
        return c // NX - block // NX, dx, jnp.where(valid, 0.0, -1e30)

    def judge(j, carry):
        later = jnp.minimum(c + j, nblk - 1)
        hit = lists[later, 0] == c
        for m in range(1, window):
            hit = hit | (lists[later, m] == c)
        hit = hit & (j < window) & (c + j < nblk)
        veto[j] = jnp.where(hit, 0.0, 1e30)
        return carry

    lax.fori_loop(0, veto.shape[0], judge, 0)
    m_buf[...] = jnp.full_like(m_buf, -jnp.inf)
    l_buf[...] = jnp.zeros_like(l_buf)
    acc[...] = jnp.zeros_like(acc)
    rsum[...] = jnp.zeros_like(rsum)

    def first(i, carry):
        for j in [i * UNROLL + u for u in range(UNROLL)]:
            s, dx, pen = entry(j)
            hits = band_hits(kw[s, dx, BLK : BLK + 16, 0:BLK].astype(F32)[0:1], 32)
            for h in range(heads):
                k_h = kw[s, dx, 0:BLK, head_cols(h)]
                score = dot(qb[0:BLK, head_cols(h)], k_h, NT) * scale + dot(ext[h], hits, NN)
                score = score + pen
                s_buf[j, h] = score
                m_buf[h] = jnp.maximum(m_buf[h], score)
        return carry

    lax.fori_loop(0, steps, first, 0)
    for h in range(heads):
        m_buf[h] = jnp.broadcast_to(jnp.max(m_buf[h], axis=1, keepdims=True), (BLK, BLK))

    def second(i, carry):
        for h in range(heads):
            total, mixed = l_buf[h], acc[h]
            for j in [i * UNROLL + u for u in range(UNROLL)]:
                s, dx, _ = entry(j)
                v_h = vw[s, dx, :, head_cols(h)]
                expo = jnp.exp(s_buf[j, h] - m_buf[h])
                total = total + expo
                mixed = mixed + dot(expo.astype(BF16), v_h, NN)
            l_buf[h] = total
            acc[h] = mixed
        return carry

    lax.fori_loop(0, steps, second, 0)
    lane = lax.broadcasted_iota(jnp.int32, (BLK, BLK), 1)
    table = jnp.zeros((BLK, BLK), F32)
    for h in range(heads):
        total = jnp.sum(l_buf[h], axis=1, keepdims=True)
        attended = (acc[h] / total).astype(BF16)
        att[:, head_cols(h)] = attended
        lse = m_buf[h] + jnp.log(total)
        g_h = gw[0:BLK, head_cols(h)].astype(F32)
        delta = jnp.sum(g_h * attended.astype(F32), axis=1, keepdims=True)
        m_buf[h] = lse
        l_buf[h] = jnp.broadcast_to(delta, (BLK, BLK))
        table = jnp.where(lane == h, lse, table)
        table = jnp.where(lane == heads + h, l_buf[h], table)
        acc[h] = jnp.zeros((BLK, HEAD), F32)
    stats[...] = jnp.transpose(table)[0:8]
    out[...] = dot(att[...], w_out[...], NN).astype(BF16)

    def third(i, carry):
        bins = rsum[...]
        for h in range(heads):
            grad = acc[h]
            for j in [i * UNROLL + u for u in range(UNROLL)]:
                s, dx, _ = entry(j)
                band_row = kw[s, dx, BLK : BLK + 16, 0:BLK].astype(F32)[0:1]
                k_h = kw[s, dx, 0:BLK, head_cols(h)]
                v_h = vw[s, dx, :, head_cols(h)]
                prob = jnp.exp(s_buf[j, h] - m_buf[h])
                dprob = dot(gw[0:BLK, head_cols(h)], v_h, NT)
                dscore = prob * (dprob - l_buf[h])
                half = dscore.astype(BF16)
                rest = (dscore - half.astype(F32)).astype(BF16)
                grad = grad + dot(half, k_h, NN)
                hits = band_hits(band_row, BLK, 8 * h)
                bins = bins + (dot(half, hits, NT) + dot(rest, hits, NT))
            acc[h] = grad
        rsum[...] = bins
        return carry

    lax.fori_loop(0, steps, third, 0)
    for h in range(heads):
        grad_q[:, head_cols(h)] = (acc[h] * scale).astype(BF16)
    own = bands[...]
    pick = (lax.broadcasted_iota(jnp.int32, (8, BLK), 0) == own).astype(F32)
    bias[...] = dot(pick, rsum[...], NN, lax.Precision.HIGHEST)


def share_kernel(
    heads, veto, partial, stats, bias, k, v, ext, qbw, gw, attn, grad_k, grad_v, total,
    pieces, window, bx, bz, mid, qv, gv, dk, dv,
    p_send, p_recv, s_send, s_recv, b_send, b_recv, local
):
    c = lax.axis_index("ctx")
    t = lax.axis_index("tp")
    d = lax.axis_index("dp")
    x = lax.rem(c, NX)
    z = c // NX
    tps = partial.shape[0]
    count = window.shape[0]
    ring = NX * NZ
    scale = 1.0 / math.sqrt(HEAD)
    q_load = pltpu.make_async_copy(qbw, qv, local.at[1])
    q_load.start()
    g_load = pltpu.make_async_copy(gw, gv, local.at[2])
    g_load.start()
    dk[...] = jnp.zeros_like(dk)
    dv[...] = jnp.zeros_like(dv)
    barrier = pltpu.get_barrier_semaphore()
    for dc in range(1, ring):
        pl.semaphore_signal(
            barrier, inc=1, device_id={"ctx": lax.rem(c + dc, ring)}, device_id_type=MESH
        )
    for dt in range(1, tps):
        pl.semaphore_signal(
            barrier, inc=1, device_id={"tp": lax.rem(t + dt, tps)}, device_id_type=MESH
        )
    for dz in range(NZ):
        far = {"ctx": lax.rem(z + dz, NZ) * NX + x, "dp": 1 - d}
        pl.semaphore_signal(barrier, inc=1, device_id=far, device_id_type=MESH)
    pl.semaphore_wait(barrier, ring - 1 + tps - 1 + NZ)

    def piece_copy(dt):
        peer = lax.rem(t + dt, tps)
        return remote(partial.at[peer], pieces.at[dt], p_send.at[dt], p_recv.at[dt], "tp", peer)

    def stat_copy(j):
        peer = jnp.clip(c - j, 0, ring - 1)
        return remote(stats, window.at[j], s_send.at[j], s_recv.at[j], "ctx", peer)

    def x_copy(dx, slot):
        peer = z * NX + lax.rem(x + dx, NX)
        return remote(bias, bx.at[slot], b_send.at[0, dx], b_recv.at[0, dx], "ctx", peer)

    def z_copy(side, dz, step):
        other = d if side == 0 else 1 - d
        peer = lax.rem(z + NZ + step * dz, NZ) * NX + x
        slot = d * NZ + z if step > 0 else other * NZ + lax.rem(z + NZ - dz, NZ)
        return pltpu.make_async_remote_copy(
            src_ref=mid,
            dst_ref=bz.at[slot],
            send_sem=b_send.at[1 + side, dz],
            recv_sem=b_recv.at[1 + side, dz],
            device_id={"ctx": peer, "dp": other},
            device_id_type=MESH,
        )

    far_pairs = [(side, dz) for side in range(2) for dz in range(NZ) if side or dz]

    for dx in range(1, NX):
        x_copy(dx, x).start()
    for j in range(1, count):

        @pl.when(c >= j)
        def _():
            stat_copy(j).start()

    for dt in range(1, tps):
        piece_copy(dt).start()
    own_piece = pltpu.make_async_copy(partial.at[t], pieces.at[0], local.at[0])
    own_piece.start()
    window[0] = stats[...]
    bx[x] = bias[...]
    for dx in range(1, NX):
        x_copy(dx, lax.rem(x + NX - dx, NX)).wait_recv()
    mid[...] = (bx[0] + bx[1]) + (bx[2] + bx[3])
    for side, dz in far_pairs:
        z_copy(side, dz, 1).start()
    bz[d * NZ + z] = mid[...]
    for j in range(1, count):

        @pl.when(c + j < ring)
        def _():
            stat_copy(j).wait_recv()

    q_load.wait()
    g_load.wait()

    def step(i, carry):
        for h in range(heads):
            k_h = k[:, head_cols(h)]
            v_h = v[:, head_cols(h)]
            sum_k, sum_v = dk[h], dv[h]
            for j in [i * UNROLL + u for u in range(UNROLL)]:
                there = c + j < jnp.minimum(c + count, ring)
                s = jnp.where(there, (x + j) // NX, 0)
                dx = jnp.where(there, lax.rem(j, NX), 0)
                rows = window[jnp.where(there, j, 0)]
                hits = band_hits(qv[s, dx, BLK : BLK + 16, 0:BLK].astype(F32)[0:1], 32)
                q_h = qv[s, dx, 0:BLK, head_cols(h)]
                g_h = gv[s, dx, :, head_cols(h)]
                score = dot(k_h, q_h, NT) * scale + dot(ext[h], hits, NN)
                prob = jnp.exp(score - (rows[h : h + 1] + veto[j]))
                dprob = dot(v_h, g_h, NT)
                dscore = prob * (dprob - rows[heads + h : heads + h + 1])
                sum_k = sum_k + dot(dscore.astype(BF16), q_h, NN)
                sum_v = sum_v + dot(prob.astype(BF16), g_h, NN)
            dk[h] = sum_k
            dv[h] = sum_v
        return carry

    lax.fori_loop(0, veto.shape[0] // UNROLL, step, 0)
    for h in range(heads):
        grad_k[:, head_cols(h)] = (dk[h] * scale).astype(BF16)
        grad_v[:, head_cols(h)] = dv[h].astype(BF16)
    own_piece.wait()
    for dt in range(1, tps):
        piece_copy(dt).wait_recv()
    out = pieces[0].astype(F32)
    for i in range(1, tps):
        out = out + pieces[i].astype(F32)
    attn[...] = out.astype(BF16)
    for side, dz in far_pairs:
        z_copy(side, dz, -1).wait_recv()
    bins = bz[0]
    for i in range(1, 2 * NZ):
        bins = bins + bz[i]
    total[...] = bins
    for dx in range(1, NX):
        x_copy(dx, x).wait_send()
    for side, dz in far_pairs:
        z_copy(side, dz, 1).wait_send()
    for j in range(1, count):

        @pl.when(c >= j)
        def _():
            stat_copy(j).wait_send()

    for dt in range(1, tps):
        piece_copy(dt).wait_send()


def write_kernel(a, b, c, a_out, b_out, c_out):
    a_out[...] = a[...]
    b_out[...] = b[...]
    c_out[...] = c[...]


def split_bands(values):
    parts = []
    rest = values
    for _ in range(3):
        part = lax.reduce_precision(rest, 8, 7)
        parts.append(part)
        rest = rest - part
    stacked = jnp.stack(parts, axis=2)
    stacked = jnp.pad(stacked, ((0, 0), (0, 0), (0, 1), (0, 8 - values.shape[2])))
    return stacked.reshape(values.shape[0], values.shape[1], 32).astype(BF16)


def body(query, key, value, w_out, output_gradient, key_blocks, band_ids, band_bias):
    q_rows, k_rows, v_rows, og = query[0], key[0], value[0], output_gradient[0]
    bands, lists = band_ids[0], key_blocks[0]
    rows, feats = q_rows.shape
    heads = band_bias.shape[0]
    window = lists.shape[1]
    width = og.shape[1]
    tps = lax.axis_size("tp")
    c = lax.axis_index("ctx")
    band_row = bands[None, :]
    one_hot = (bands[:, None] == jnp.arange(band_bias.shape[1], dtype=jnp.int32)).astype(F32)
    high = lax.Precision.HIGHEST
    ext_q = split_bands(jnp.einsum("ia,hab->hib", one_hot, band_bias, precision=high))
    ext_k = split_bands(jnp.einsum("kb,hab->hka", one_hot, band_bias, precision=high))
    extra = -window % UNROLL

    vmem = pl.BlockSpec(memory_space=pltpu.VMEM)
    smem = pl.BlockSpec(memory_space=pltpu.SMEM)
    hbm = pl.BlockSpec(memory_space=pl.ANY)
    shape = jax.ShapeDtypeStruct
    qb_shape = (rows + 16, feats)
    kw, vw, qbw, gw, grad_att = pl.pallas_call(
        exchange_kernel,
        out_shape=(
            shape((NX + 1, NX) + qb_shape, BF16),
            shape((NX + 1, NX, rows, feats), BF16),
            shape((NX + 1, NX) + qb_shape, BF16),
            shape((NX + 1, NX, rows, feats), BF16),
            shape((rows, feats), BF16),
        ),
        in_specs=[vmem] * 5 + [hbm],
        out_specs=(hbm, hbm, hbm, hbm, vmem),
        scratch_shapes=[
            pltpu.VMEM(qb_shape, BF16),
            pltpu.VMEM(qb_shape, BF16),
            pltpu.VMEM((tps,) + og.shape, BF16),
            pltpu.VMEM(w_out.shape, BF16),
            pltpu.SemaphoreType.DMA((4, NX + 1, NX)),
            pltpu.SemaphoreType.DMA((4, NX + 1, NX)),
            pltpu.SemaphoreType.DMA((tps,)),
            pltpu.SemaphoreType.DMA((tps,)),
            pltpu.SemaphoreType.DMA((5,)),
        ],
        compiler_params=pltpu.CompilerParams(collective_id=0, has_side_effects=True),
        name="exchange",
    )(q_rows, k_rows, v_rows, band_row, og, w_out)

    square = pltpu.VMEM((heads, BLK, BLK), F32)
    partial, grad_q, stats, bias, veto = pl.pallas_call(
        functools.partial(query_kernel, heads),
        out_shape=(
            shape((rows, width), BF16),
            shape((rows, feats), BF16),
            shape((8, BLK), F32),
            shape((8, BLK), F32),
            shape((window + extra,), F32),
        ),
        in_specs=[smem] + [vmem] * 7,
        out_specs=(vmem,) * 4 + (smem,),
        scratch_shapes=[
            pltpu.VMEM((window + extra, heads, BLK, BLK), F32),
            square,
            square,
            square,
            pltpu.VMEM((BLK, BLK), F32),
            pltpu.VMEM((rows, feats), BF16),
        ],
        name="query_side",
    )(lists, kw, vw, q_rows, band_row, grad_att, ext_q, w_out)

    tile = (8, BLK)
    attn_out, grad_k, grad_v, bias_total = pl.pallas_call(
        functools.partial(share_kernel, heads),
        out_shape=(
            shape(og.shape, BF16),
            shape((rows, feats), BF16),
            shape((rows, feats), BF16),
            shape(tile, F32),
        ),
        in_specs=[smem] + [vmem] * 6 + [hbm] * 2,
        out_specs=(vmem,) * 4,
        scratch_shapes=[
            pltpu.VMEM((tps,) + og.shape, BF16),
            pltpu.VMEM((window,) + tile, F32),
            pltpu.VMEM((NX,) + tile, F32),
            pltpu.VMEM((2 * NZ,) + tile, F32),
            pltpu.VMEM(tile, F32),
            pltpu.VMEM(qbw.shape, BF16),
            pltpu.VMEM(gw.shape, BF16),
            square,
            square,
            pltpu.SemaphoreType.DMA((tps,)),
            pltpu.SemaphoreType.DMA((tps,)),
            pltpu.SemaphoreType.DMA((window,)),
            pltpu.SemaphoreType.DMA((window,)),
            pltpu.SemaphoreType.DMA((3, NZ)),
            pltpu.SemaphoreType.DMA((3, NZ)),
            pltpu.SemaphoreType.DMA((3,)),
        ],
        compiler_params=pltpu.CompilerParams(collective_id=1, has_side_effects=True),
        name="share",
    )(
        veto, partial.reshape((tps,) + og.shape), stats, bias,
        k_rows, v_rows, ext_k, qbw, gw,
    )

    attn_out, grad_k, grad_v = pl.pallas_call(
        write_kernel,
        out_shape=(shape(og.shape, BF16), shape((rows, feats), BF16), shape((rows, feats), BF16)),
        in_specs=[vmem] * 3,
        out_specs=(vmem,) * 3,
        name="write_out",
    )(attn_out, grad_k, grad_v)

    na, nb = band_bias.shape[1:]
    grad_bias = bias_total[:na, : 8 * heads].reshape(na, heads, 8)[:, :, :nb].transpose(1, 0, 2)
    return (attn_out[None], grad_q[None], grad_k[None], grad_v[None], grad_bias)


def solution(mesh):
    return jax.shard_map(
        body,
        mesh=mesh,
        in_specs=(
            P("dp", "ctx", "tp"),
            P("dp", "ctx", "tp"),
            P("dp", "ctx", "tp"),
            P("tp", None),
            P("dp", ("ctx", "tp"), None),
            P("dp", None, None),
            P("dp", "ctx"),
            P("tp", None, None),
        ),
        out_specs=(
            P("dp", ("ctx", "tp"), None),
            P("dp", "ctx", "tp"),
            P("dp", "ctx", "tp"),
            P("dp", "ctx", "tp"),
            P("tp", None, None),
        ),
        check_vma=False,
    )
```
